32 devices in a mesh: comp: 8 (over y, x, core), tile: 4 (over z).
Axes of the slice: x: 2, y: 2, z: 4, core: 2. Of those that a mesh axis runs over, the one named last changes fastest.
Arguments:
- atm_state: float32 [128, 128, 512], P(None, 'comp', 'tile'), may hold values from -6 to 6
- ocean_state: float32 [48, 128, 512], P(None, 'comp', 'tile'), may hold values from -6 to 6
- atm_rate: float32 [128], replicated, may hold values from 0.02 to 0.24
- ocean_rate: float32 [48], replicated, may hold values from 0.02 to 0.24
- ocean_mask: int32 [128, 4], P('comp', 'tile'), may hold values 0 or 1
- remap_weight: bfloat16 [8, 192, 128, 128], P('comp', 'tile'), may hold values from -0.5 to 0.5
- pair_src: int32 [8, 192], P('comp', 'tile'), may hold values from 0 to 63, as said below
- pair_tgt: int32 [8, 192], P('comp', 'tile'), may hold values from 0 to 63, as said below
- pair_count: int32 [8, 4], P('comp', 'tile'), may hold values from 24 to 48, as said below
Outputs:
- atm_next: float32 [128, 128, 512], P(None, 'comp', 'tile')
- ocean_next: float32 [48, 128, 512], P(None, 'comp', 'tile')
The draws below stay inside these ranges and needn't reach their ends.
Inputs may be any that keep to these rules, and one draw needn't show every extreme that they name: `pair_src`: entry d * 48 + j of row b names atmosphere tile e * 16 + y of band b. Among the first pair_count[b, d] entries of device d at most 13 have the same e, and every device has 13 live entries with one same e. `pair_tgt`: entry d * 48 + j of row b names ocean tile e * 16 + y of band b. Among the first pair_count[b, d] entries of device d at most 13 have the same e, and every device has 13 live entries with one same e. `pair_count`: each row b has some device with 48 live slots.
All inputs are finite; a program needn't handle non-finite values. No bound on the sum of `ocean_mask` on one device may be relied on, other than what follows from the above.
Results may differ from the reference program's by a relative error of at most 0.002.
Values may be sent and summed in bfloat16 or wider, within the bound.
No kernel may reach another device: no remote copies, remote signals or barrier semaphores. Data moves between devices by JAX's collectives and lax.ppermute only.
A program may use at most 64 MiB of HBM per device.

```python
import math
import jax
import jax.numpy as jnp
from jax import lax

SURF = 8
TILE = 128
AY = 16
OY = 16
PAIRS = 48
CAP = 13
CH_A = 128
CH_O = 48
NY = 128
NOY = 128
NX = 512
N_COMP = 8
N_TILE = 4


def routed_tiles(base_key, salt_value, row_count):
    salted = jax.random.fold_in(base_key, salt_value)
    first_key, second_key, third_key = jax.random.split(salted, 3)
    slot_total = N_TILE * CAP
    slot_index = jnp.arange(slot_total, dtype=jnp.int32)
    raw_score = jax.random.randint(first_key, (N_COMP, N_TILE, slot_total), 0, 1 << 16)
    full_peer = jax.random.randint(second_key, (N_COMP, N_TILE, 1), 0, N_TILE)
    ordered = jnp.where(slot_index // CAP == full_peer, slot_index - slot_total, raw_score * slot_total + slot_index)
    chosen = jnp.argsort(ordered, axis=-1, stable=True)[..., :PAIRS].astype(jnp.int32)
    offset = jax.random.randint(third_key, (N_COMP, N_TILE, PAIRS), 0, row_count)
    return (chosen // CAP * row_count + offset).reshape(N_COMP, N_TILE * PAIRS).astype(jnp.int32)


def draw_pair_src(key, part):
    return routed_tiles(key, 11, AY)


def draw_pair_tgt(key, part):
    return routed_tiles(key, 23, OY)


def draw_pair_count(key, part):
    salted = jax.random.fold_in(key, 37)
    first_key, second_key = jax.random.split(salted, 2)
    lowest = max(CAP, PAIRS // 2)
    spread_total = PAIRS - lowest
    raw_value = jax.random.randint(first_key, (N_COMP, N_TILE), 0, spread_total + 1)
    counted = lowest + raw_value * raw_value // max(spread_total, 1)
    busiest = jax.random.randint(second_key, (N_COMP, 1), 0, N_TILE)
    device_index = jnp.arange(N_TILE, dtype=jnp.int32)[None, :]
    return jnp.where(device_index == busiest, PAIRS, jnp.minimum(counted, PAIRS)).astype(jnp.int32)


def plant(array, key, low, top_value):
    longest = array.shape.index(max(array.shape))
    spots = []
    for shift in (0, 1):
        where = [jax.random.randint(jax.random.fold_in(key, axis), (), 0, length) for axis, length in enumerate(array.shape)]
        where[longest] = (where[longest] + shift) % array.shape[longest]
        spots.append(tuple(where))
    return array.at[spots[0]].set(low).at[spots[1]].set(top_value)


def level_of(own_key, shape, shards, low, largest):
    loudness, own = 1.0, jax.random.fold_in(own_key, 6)
    for axis_at, blocks in shards:
        draws = jnp.exp(jax.random.uniform(jax.random.fold_in(own, axis_at), (blocks,), jnp.float32, low / len(shards), largest / len(shards)))
        loudness = loudness * jnp.repeat(draws, shape[axis_at] // blocks).reshape([-1 if axis == axis_at else 1 for axis in range(len(shape))])
    return loudness


def centred(stream_key, extent, deviation, most, cuts=(), kind=jnp.bfloat16):
    entries = deviation * jax.random.normal(stream_key, extent, jnp.float32)
    if cuts:
        entries = entries * level_of(stream_key, extent, cuts, -0.22, 0.18)
    return jnp.clip(entries, -most, most).astype(kind)


def setup_inputs(seed: int = 0) -> dict:
    key_list = jax.random.split(jax.random.key(seed), 10)
    return {
        "atm_state": centred(key_list[0], (CH_A, NY, NX), 1.0, 6.0, ((1, 8), (2, 4)), jnp.float32),
        "ocean_state": centred(key_list[1], (CH_O, NOY, NX), 1.0, 6.0, ((1, 8), (2, 4)), jnp.float32),
        "atm_rate": jnp.clip(jnp.exp(jax.random.uniform(key_list[2], (CH_A,), jnp.float32, math.log(0.02), math.log(0.24))), 0.02, 0.24),
        "ocean_rate": jnp.clip(jnp.exp(jax.random.uniform(key_list[3], (CH_O,), jnp.float32, math.log(0.02), math.log(0.24))), 0.02, 0.24),
        "ocean_mask": plant((jax.random.randint(key_list[4], (NOY, N_TILE), 0, 4) < 3).astype(jnp.int32), jax.random.fold_in(key_list[4], 1), 0, 1),
        "remap_weight": centred(key_list[5], (N_COMP, N_TILE * PAIRS, TILE, TILE), TILE ** -0.5, 0.5, ((0, 8), (1, 4))),
        "pair_src": draw_pair_src(jax.random.fold_in(key_list[9], 71), 0),
        "pair_tgt": draw_pair_tgt(jax.random.fold_in(key_list[9], 71), 0),
        "pair_count": draw_pair_count(jax.random.fold_in(key_list[9], 71), 0),
    }


def relax(values, spread):
    padded = jnp.pad(values, ((0, 0), (1, 1), (0, 0)))
    beside_all = padded[:, 2:] + padded[:, :-2] + jnp.roll(values, 1, 2) + jnp.roll(values, -1, 2)
    return values + spread[:, None, None] * (beside_all - 4.0 * values)


def to_tiles(values, row_count):
    shaped = values.reshape(SURF, N_COMP, row_count, N_TILE, TILE)
    return shaped.transpose(1, 3, 2, 0, 4).reshape(N_COMP, N_TILE * row_count, SURF, TILE)


def from_tiles(values, row_count):
    shaped = values.reshape(N_COMP, N_TILE, row_count, SURF, TILE)
    return shaped.transpose(3, 0, 2, 1, 4).reshape(SURF, N_COMP * row_count, N_TILE * TILE)


def reference(atm_state, ocean_state, atm_rate, ocean_rate, ocean_mask, remap_weight, pair_src, pair_tgt, pair_count):
    wet = jnp.repeat(ocean_mask.astype(jnp.float32), TILE, axis=1)
    atm_source = atm_state[:SURF].astype(jnp.bfloat16)
    ocean_source = (ocean_state[:SURF] * wet[None]).astype(jnp.bfloat16)
    atm_tiles = to_tiles(atm_source, AY)
    ocean_tiles = to_tiles(ocean_source, OY)

    def couple(inputs):
        atm_group, ocean_group, weights, anchor, target, live_count = inputs
        active = (jnp.arange(PAIRS)[None, :] < live_count[:, None]).reshape(-1).astype(jnp.float32)
        blocks = weights.astype(jnp.float32)
        forward = jnp.einsum("pft,pts->pfs", atm_group[anchor].astype(jnp.float32), blocks,
                             precision=lax.Precision.HIGHEST) * active[:, None, None]
        reverse = jnp.einsum("pfs,pts->pft", ocean_group[target].astype(jnp.float32), blocks,
                             precision=lax.Precision.HIGHEST) * active[:, None, None]
        ocean_force = jnp.zeros((N_TILE * OY, SURF, TILE), jnp.float32).at[target].add(forward)
        atm_force = jnp.zeros((N_TILE * AY, SURF, TILE), jnp.float32).at[anchor].add(reverse)
        return atm_force, ocean_force

    atm_force, ocean_force = lax.map(couple, (atm_tiles, ocean_tiles, remap_weight, pair_src, pair_tgt, pair_count))
    atm_forcing = from_tiles(atm_force, AY)
    ocean_forcing = from_tiles(ocean_force, OY)
    atm_stepped = relax(relax(atm_state, atm_rate), atm_rate)
    ocean_stepped = relax(relax(ocean_state, ocean_rate), ocean_rate)
    atm_next = atm_stepped.at[:SURF].add(atm_forcing)
    ocean_next = ocean_stepped.at[:SURF].add(ocean_forcing * wet[None])
    return atm_next, ocean_next
```

```python
import functools

import jax
import jax.numpy as jnp
from jax import lax
from jax.experimental import pallas as pl
from jax.experimental.pallas import tpu as pltpu
from jax.sharding import PartitionSpec as P

SURF = 8
F32 = jnp.float32
BF16 = jnp.bfloat16
VMEM = pl.BlockSpec(memory_space=pltpu.VMEM)
SMEM = pl.BlockSpec(memory_space=pltpu.SMEM)


def beside_even(index):
    return index + 1 - 2 * (index % 2)


def beside_odd(index, count):
    return (index - 1 + 2 * (index % 2) + count) % count


def tile_pairs(count):
    routes = [
        [(i, beside_even(i)) for i in range(count)],
        [(i, beside_odd(i, count)) for i in range(count)],
    ]
    routes += [[(i, (i + s) % count) for i in range(count)] for s in range(2, count - 1)]
    return routes


def peers(me, count):
    a = beside_even(me)
    b = beside_odd(me, count)
    far = range(2, count - 1)
    sources = [a, b] + [lax.rem(me - s + count, count) for s in far]
    targets = [a, b] + [lax.rem(me + s, count) for s in far]
    return sources, targets


def comp_pairs(count):
    even = [(i, beside_even(i)) for i in range(count)]
    odd = [(i, i + 1) for i in range(1, count - 1, 2)] + [(i + 1, i) for i in range(1, count - 1, 2)]
    return even, odd


def pack_surface(mask, atm, ocean, out):
    rows_a = atm.shape[1]
    rows_o = ocean.shape[1]
    for y in range(rows_a):
        out[y] = atm[:, y, :].astype(BF16)
    for y in range(rows_o):
        out[rows_a + y] = (ocean[:, y, :] * mask[y, 0].astype(F32)).astype(BF16)


def pack_rows(rows, atm, ocean, even_out, odd_out):
    parity = lax.rem(lax.axis_index("comp"), 2)
    at = 0
    for ref in (atm, ocean):
        channels = ref.shape[0] // rows
        for c in range(0, channels, 8):
            for r in range(2):
                low = ref[pl.ds(c * rows + r, 8, stride=rows), :]
                high = ref[pl.ds(c * rows + rows - 2 + r, 8, stride=rows), :]
                even_out[r, at + c : at + c + 8, :] = jnp.where(parity == 0, high, low).astype(BF16)
                odd_out[r, at + c : at + c + 8, :] = jnp.where(parity == 0, low, high).astype(BF16)
        at += channels


def halo_rows(parity, even_in, odd_in, at):
    e = [even_in[r, at : at + 8, :].astype(F32) for r in range(2)]
    o = [odd_in[r, at : at + 8, :].astype(F32) for r in range(2)]
    north = [jnp.where(parity == 0, o[r], e[r]) for r in range(2)]
    south = [jnp.where(parity == 0, e[r], o[r]) for r in range(2)]
    return north, south


def pack_columns(rows, atm, ocean, atm_rate, ocean_rate, even_in, odd_in, out_a, out_b, edge, inner, stage):
    parity = lax.rem(lax.axis_index("comp"), 2)
    tile_parity = lax.rem(lax.axis_index("tile"), 2)
    lanes = atm.shape[1]
    row = lax.broadcasted_iota(jnp.int32, (8, lanes), 0)
    lane = lax.broadcasted_iota(jnp.int32, (8, lanes), 1)
    east = lax.div(row, 2) == tile_parity
    outer_lane = jnp.where(east, lanes - 1, 0)
    inner_lane = jnp.where(east, lanes - 2, 1)
    first = lax.rem(row, 2) == 0
    live = row < 4
    pick_edge = jnp.where(live & first & (lane == outer_lane), 1.0, 0.0).astype(BF16)
    pick_inner = jnp.where(
        live & (lane == jnp.where(first, inner_lane, outer_lane)), 1.0, 0.0
    ).astype(BF16)
    dims = (((1,), (1,)), ((), ()))
    stage[...] = jnp.zeros_like(stage)
    at = 0
    for ref, rate in ((atm, atm_rate), (ocean, ocean_rate)):
        channels = ref.shape[0] // rows
        for c in range(0, channels, 8):
            rho = rate[c : c + 8, :]
            north, south = halo_rows(parity, even_in, odd_in, at + c)
            q = [north[1]]
            q += [ref[pl.ds(c * rows + r, 8, stride=rows), :] for r in range(rows)]
            q += [south[0]]
            for r in range(rows):
                mid = (1.0 - 4.0 * rho) * q[r + 1] + rho * (q[r] + q[r + 2])
                edge[pl.ds(r, 8, stride=rows), :] = 2.0 * rho * mid
                inner[pl.ds(r, 8, stride=rows), :] = rho * rho * q[r + 1]
            found = lax.dot_general(
                pick_edge, edge[...].astype(BF16), dims, preferred_element_type=F32
            ) + lax.dot_general(
                pick_inner, inner[...].astype(BF16), dims, preferred_element_type=F32
            )
            j = (at + c) // 8
            stage[0, 2 * j : 2 * j + 2, :] = found[0:2, :]
            stage[1, 2 * j : 2 * j + 2, :] = found[2:4, :]
        at += channels
    out_a[...] = stage[0].astype(BF16)
    out_b[...] = stage[1].astype(BF16)


def remap(tile_count, rows_a, rows_o, *refs):
    src, tgt, number, weights, own = refs[:5]
    got = refs[5 : 5 + tile_count - 1]
    own_out = refs[5 + tile_count - 1]
    outs = refs[6 + tile_count - 1 : 6 + 2 * (tile_count - 1)]
    band, total = refs[6 + 2 * (tile_count - 1) :]
    me = lax.axis_index("tile")
    block = rows_a + rows_o
    sources, targets = peers(me, tile_count)
    band[pl.ds(me * block, block)] = own[...]
    for e, ref in zip(sources, got):
        band[pl.ds(e * block, block)] = ref[...]
    total[...] = jnp.zeros_like(total)
    pairs = weights.shape[0]
    live_count = number[0, 0]
    trans = (((1,), (1,)), ((), ()))
    plain = (((1,), (0,)), ((), ()))
    group = 8
    for start in range(0, pairs, group):
        made = []
        for k in range(start, min(start + group, pairs)):
            a = src[0, k]
            o = tgt[0, k]
            at_a = lax.div(a, rows_a) * block + lax.rem(a, rows_a)
            at_o = lax.div(o, rows_o) * block + rows_a + lax.rem(o, rows_o)
            live = k < live_count
            w = weights[k]
            ta = band[at_a]
            to = band[at_o]
            ta = jnp.where(live, ta, jnp.zeros_like(ta))
            to = jnp.where(live, to, jnp.zeros_like(to))
            ahead = lax.dot_general(ta, w, plain, preferred_element_type=F32)
            back = lax.dot_general(to, w, trans, preferred_element_type=F32)
            made.append((at_a, at_o, ahead, back))
        for at_a, at_o, ahead, back in made:
            total[at_o] += ahead
            total[at_a] += back
    own_out[...] = total[pl.ds(me * block, block)]
    for e, ref in zip(targets, outs):
        ref[...] = total[pl.ds(e * block, block)].astype(BF16)


def stencil(rows, atm, ocean, atm_rate, ocean_rate, even_in, odd_in, atm_out, ocean_out):
    comp = lax.axis_index("comp")
    parity = lax.rem(comp, 2)
    lanes = atm.shape[1]
    lane = lax.broadcasted_iota(jnp.int32, (8, lanes), 1)
    at_west = lane == 0
    at_east = lane == lanes - 1
    keep_north = jnp.where(comp == 0, 0.0, 1.0).astype(F32)
    keep_south = jnp.where(comp == lax.axis_size("comp") - 1, 0.0, 1.0).astype(F32)
    at = 0
    for ref, rate, out in ((atm, atm_rate, atm_out), (ocean, ocean_rate, ocean_out)):
        channels = ref.shape[0] // rows
        for c in range(0, channels, 8):
            rho = jnp.broadcast_to(rate[c : c + 8, :], (8, lanes))
            own = 1.0 - 4.0 * rho
            north, south = halo_rows(parity, even_in, odd_in, at + c)
            q = north + [ref[pl.ds(c * rows + r, 8, stride=rows), :] for r in range(rows)] + south
            p = []
            for i in range(1, rows + 3):
                west = jnp.where(at_west, 0.0, pltpu.roll(q[i], 1, 1))
                east = jnp.where(at_east, 0.0, pltpu.roll(q[i], lanes - 1, 1))
                p.append(own * q[i] + rho * ((q[i - 1] + q[i + 1]) + (west + east)))
            p[0] = p[0] * keep_north
            p[rows + 1] = p[rows + 1] * keep_south
            for r in range(rows):
                ghost = rho * q[r + 2]
                west = jnp.where(at_west, ghost, pltpu.roll(p[r + 1], 1, 1))
                east = jnp.where(at_east, ghost, pltpu.roll(p[r + 1], lanes - 1, 1))
                out[pl.ds(c * rows + r, 8, stride=rows), :] = own * p[r + 1] + rho * (
                    (p[r] + p[r + 2]) + (west + east)
                )
        at += channels


def final(tile_count, rows_a, rows_o, message, *refs):
    mask, atm, ocean, own = refs[:4]
    got = refs[4 : 4 + tile_count - 1]
    atm_out, ocean_out, force = refs[4 + tile_count - 1 :]
    lanes = atm.shape[1]
    tile_parity = lax.rem(lax.axis_index("tile"), 2)
    row = lax.broadcasted_iota(jnp.int32, (8, lanes), 0)
    lane = lax.broadcasted_iota(jnp.int32, (8, lanes), 1)
    east = lax.div(row, 2) == tile_parity
    spot = jnp.where(
        lax.rem(row, 2) == 0,
        jnp.where(east, lanes - 1, 0),
        jnp.where(east, lanes - 2, 1),
    )
    place = jnp.where((row < 4) & (lane == spot), 1.0, 0.0).astype(BF16)
    block = rows_a + rows_o
    for y in range(block):
        total = own[y]
        for ref in got:
            total = total + ref[8 * y : 8 * y + 8, :].astype(F32)
        if y >= rows_a:
            total = total * mask[y - rows_a, 0].astype(F32)
        start = y if y < rows_a else SURF * rows_a + y - rows_a
        force[pl.ds(start, SURF, stride=rows_a if y < rows_a else rows_o), :] = total
    dims = (((0,), (0,)), ((), ()))
    at = 0
    for ref, out, rows, add in (
        (atm, atm_out, rows_a, 0),
        (ocean, ocean_out, rows_o, SURF * rows_a),
    ):
        for c in range(0, ref.shape[0] // rows, 8):
            j = message + 2 * ((at + c) // 8)
            sides = jnp.concatenate(
                [
                    got[0][j : j + 2, :].astype(F32),
                    got[1][j : j + 2, :].astype(F32),
                    jnp.zeros((4, lanes), F32),
                ],
                axis=0,
            ).astype(BF16)
            value = ref[c * rows : (c + 8) * rows, :] + lax.dot_general(
                sides, place, dims, preferred_element_type=F32
            )
            if c == 0:
                value = value + force[add : add + SURF * rows, :]
            out[c * rows : (c + 8) * rows, :] = value
        at += ref.shape[0] // rows


def params(limit=None):
    return pltpu.CompilerParams(vmem_limit_bytes=limit)


def shards(
    atm_state,
    ocean_state,
    atm_rate,
    ocean_rate,
    ocean_mask,
    remap_weight,
    pair_src,
    pair_tgt,
    pair_count,
):
    channels_a, rows_a, lanes = atm_state.shape
    channels_o, rows_o, _ = ocean_state.shape
    channels = channels_a + channels_o
    tile_count = lax.axis_size("tile")
    block = rows_a + rows_o
    message = block * SURF
    extra = -(-2 * channels // 8 // 16) * 16
    atm = atm_state.reshape(channels_a * rows_a, lanes)
    ocean = ocean_state.reshape(channels_o * rows_o, lanes)
    rate_a = atm_rate.reshape(channels_a, 1)
    rate_o = ocean_rate.reshape(channels_o, 1)
    routes = tile_pairs(tile_count)
    even_pairs, odd_pairs = comp_pairs(lax.axis_size("comp"))

    surface = pl.pallas_call(
        pack_surface,
        grid=(1,),
        in_specs=[
            SMEM,
            pl.BlockSpec((SURF, rows_a, lanes), lambda i: (0, 0, 0)),
            pl.BlockSpec((SURF, rows_o, lanes), lambda i: (0, 0, 0)),
        ],
        out_specs=pl.BlockSpec((block, SURF, lanes), lambda i: (0, 0, 0)),
        out_shape=jax.ShapeDtypeStruct((block, SURF, lanes), BF16),
        compiler_params=params(4 << 20),
    )(ocean_mask, atm_state, ocean_state)
    far_first = list(range(len(routes)))[::-1]
    received = {}
    for i in far_first:
        received[i] = lax.ppermute(surface, "tile", routes[i])

    halo = jax.ShapeDtypeStruct((2, channels, lanes), BF16)
    even_rows, odd_rows = pl.pallas_call(
        functools.partial(pack_rows, rows_a),
        in_specs=[VMEM, VMEM],
        out_specs=[VMEM, VMEM],
        out_shape=[halo, halo],
        compiler_params=params(8 << 20),
    )(atm, ocean)
    even_in = lax.ppermute(even_rows, "comp", even_pairs)
    odd_in = lax.ppermute(odd_rows, "comp", odd_pairs)

    part = jax.ShapeDtypeStruct((block, SURF, lanes), BF16)
    results = pl.pallas_call(
        functools.partial(remap, tile_count, rows_a, rows_o),
        in_specs=[SMEM, SMEM, SMEM] + [VMEM] * (1 + tile_count),
        out_specs=[VMEM] * tile_count,
        out_shape=[jax.ShapeDtypeStruct((block, SURF, lanes), F32)] + [part] * (tile_count - 1),
        scratch_shapes=[
            pltpu.VMEM((tile_count * block, SURF, lanes), BF16),
            pltpu.VMEM((tile_count * block, SURF, lanes), F32),
        ],
        compiler_params=params(12 << 20),
    )(
        pair_src,
        pair_tgt,
        pair_count,
        remap_weight[0],
        surface,
        *[received[i] for i in range(tile_count - 1)],
    )
    own_part, parts = results[0], [p.reshape(message, lanes) for p in results[1:]]

    col_a, col_b = pl.pallas_call(
        functools.partial(pack_columns, rows_a),
        in_specs=[VMEM] * 6,
        out_specs=[VMEM, VMEM],
        out_shape=[jax.ShapeDtypeStruct((extra, lanes), BF16)] * 2,
        scratch_shapes=[
            pltpu.VMEM((8 * rows_a, lanes), F32),
            pltpu.VMEM((8 * rows_a, lanes), F32),
            pltpu.VMEM((2, extra, lanes), F32),
        ],
        compiler_params=params(8 << 20),
    )(atm, ocean, rate_a, rate_o, even_in, odd_in)
    send = [
        jnp.concatenate([parts[0], col_a], axis=0),
        jnp.concatenate([parts[1], col_b], axis=0),
    ] + parts[2:]
    returned = {}
    for i in far_first:
        returned[i] = lax.ppermute(send[i], "tile", routes[i])

    atm_base, ocean_base = pl.pallas_call(
        functools.partial(stencil, rows_a),
        in_specs=[VMEM] * 6,
        out_specs=[VMEM, VMEM],
        out_shape=[
            jax.ShapeDtypeStruct(atm.shape, F32),
            jax.ShapeDtypeStruct(ocean.shape, F32),
        ],
        compiler_params=params(8 << 20),
    )(atm, ocean, rate_a, rate_o, even_in, odd_in)

    atm_next, ocean_next = pl.pallas_call(
        functools.partial(final, tile_count, rows_a, rows_o, message),
        in_specs=[SMEM] + [VMEM] * (2 + tile_count),
        out_specs=[VMEM, VMEM],
        out_shape=[
            jax.ShapeDtypeStruct(atm.shape, F32),
            jax.ShapeDtypeStruct(ocean.shape, F32),
        ],
        scratch_shapes=[pltpu.VMEM((SURF * block, lanes), F32)],
        compiler_params=params(12 << 20),
    )(ocean_mask, atm_base, ocean_base, own_part, *[returned[i] for i in range(tile_count - 1)])
    return (
        atm_next.reshape(channels_a, rows_a, lanes),
        ocean_next.reshape(channels_o, rows_o, lanes),
    )


def solution(mesh):
    return jax.shard_map(
        shards,
        mesh=mesh,
        in_specs=(
            P(None, "comp", "tile"),
            P(None, "comp", "tile"),
            P(),
            P(),
            P("comp", "tile"),
            P("comp", "tile", None, None),
            P("comp", "tile"),
            P("comp", "tile"),
            P("comp", "tile"),
        ),
        out_specs=(P(None, "comp", "tile"), P(None, "comp", "tile")),
        check_vma=False,
    )
```

```python
import functools

import jax
import jax.numpy as jnp
from jax import lax
from jax.experimental import pallas as pl
from jax.experimental.pallas import tpu as pltpu
from jax.sharding import PartitionSpec as P

SURF = 8
F32 = jnp.float32
BF16 = jnp.bfloat16
VMEM = pl.BlockSpec(memory_space=pltpu.VMEM)
SMEM = pl.BlockSpec(memory_space=pltpu.SMEM)
HBM = pl.BlockSpec(memory_space=pltpu.HBM)
ANY = pl.BlockSpec(memory_space=pl.ANY)


def beside_even(index):
    return index + 1 - 2 * (index % 2)


def beside_odd(index, count):
    return (index - 1 + 2 * (index % 2) + count) % count


def tile_pairs(count):
    routes = [
        [(i, beside_even(i)) for i in range(count)],
        [(i, beside_odd(i, count)) for i in range(count)],
    ]
    routes += [[(i, (i + s) % count) for i in range(count)] for s in range(2, count - 1)]
    return routes


def peers(me, count):
    a = beside_even(me)
    b = beside_odd(me, count)
    far = range(2, count - 1)
    sources = [a, b] + [lax.rem(me - s + count, count) for s in far]
    targets = [a, b] + [lax.rem(me + s, count) for s in far]
    return sources, targets


def comp_pairs(count):
    even = [(i, beside_even(i)) for i in range(count)]
    odd = [(i, i + 1) for i in range(1, count - 1, 2)] + [(i + 1, i) for i in range(1, count - 1, 2)]
    return even, odd


def pack_surface(rows_a, rows_o, mask, atm, ocean, out, wet, atm_part, ocean_part, done):
    copies = [
        pltpu.make_async_copy(mask, wet, done.at[0]),
        pltpu.make_async_copy(atm.at[0 : SURF * rows_a], atm_part, done.at[1]),
        pltpu.make_async_copy(ocean.at[0 : SURF * rows_o], ocean_part, done.at[2]),
    ]
    for copy in copies:
        copy.start()
    copies[1].wait()
    for y in range(rows_a):
        out[y] = atm_part[pl.ds(y, SURF, stride=rows_a), :].astype(BF16)
    copies[0].wait()
    copies[2].wait()
    for y in range(rows_o):
        tile = ocean_part[pl.ds(y, SURF, stride=rows_o), :]
        out[rows_a + y] = (tile * wet[0, y].astype(F32)).astype(BF16)


def prepare(rows_a, rows_o, anchor, atm, ocean, rate_a, rate_o, src, tgt, number, even_out, odd_out, table, rate):
    del anchor
    parity = lax.rem(lax.axis_index("comp"), 2)
    lanes = atm.shape[1]
    at = 0
    for ref, rows in ((atm, rows_a), (ocean, rows_o)):
        channels = ref.shape[0] // rows
        for c in range(0, channels, 8):
            for r in range(2):
                low = ref[pl.ds(c * rows + r, 8, stride=rows), :]
                high = ref[pl.ds(c * rows + rows - 2 + r, 8, stride=rows), :]
                even_out[r, at + c : at + c + 8, :] = jnp.where(parity == 0, high, low).astype(BF16)
                odd_out[r, at + c : at + c + 8, :] = jnp.where(parity == 0, low, high).astype(BF16)
        at += channels
    split = rate_a.shape[1]
    rate[0:split, :] = jnp.broadcast_to(rate_a[...], (lanes, split)).T
    rate[split:, :] = jnp.broadcast_to(rate_o[...], (lanes, rate_o.shape[1])).T
    block = rows_a + rows_o
    pairs = src.shape[1]
    table[0:1, 0:pairs] = lax.div(src[...], rows_a) * block + lax.rem(src[...], rows_a)
    table[1:2, 0:pairs] = lax.div(tgt[...], rows_o) * block + rows_a + lax.rem(tgt[...], rows_o)
    table[2:3, 0:1] = number[...]


def halo_rows(parity, even_in, odd_in, at):
    e = [even_in[r, at : at + 8, :].astype(F32) for r in range(2)]
    o = [odd_in[r, at : at + 8, :].astype(F32) for r in range(2)]
    north = [jnp.where(parity == 0, o[r], e[r]) for r in range(2)]
    south = [jnp.where(parity == 0, e[r], o[r]) for r in range(2)]
    return north, south


def pack_columns(rows_a, rows_o, atm, ocean, rate, even_in, odd_in, out_a, out_b, spread, stage):
    parity = lax.rem(lax.axis_index("comp"), 2)
    tile_parity = lax.rem(lax.axis_index("tile"), 2)
    lanes = atm.shape[1]
    row = lax.broadcasted_iota(jnp.int32, (8, lanes), 0)
    lane = lax.broadcasted_iota(jnp.int32, (8, lanes), 1)
    east = lax.div(row, 2) == tile_parity
    second = lax.rem(row, 2)
    spot = jnp.where(east, lanes - 1 - second, second)
    pick = jnp.where((row < 4) & (lane == spot), 1.0, 0.0).astype(BF16)
    outer = (lane == 0) | (lane == lanes - 1)
    turn = (lane == 1) | (lane == lanes - 1)
    dims = (((1,), (1,)), ((), ()))
    stage[...] = jnp.zeros_like(stage)
    at = 0
    for ref, rows in ((atm, rows_a), (ocean, rows_o)):
        channels = ref.shape[0] // rows
        for c in range(0, channels, 8):
            rho = rate[at + c : at + c + 8, :]
            own = 2.0 * rho * (1.0 - 4.0 * rho)
            square = rho * rho
            north, south = halo_rows(parity, even_in, odd_in, at + c)
            q = [north[1]]
            q += [ref[pl.ds(c * rows + r, 8, stride=rows), :] for r in range(rows)]
            q += [south[0]]
            for r in range(rows):
                far = square * q[r + 1]
                near = own * q[r + 1] + 2.0 * square * (q[r] + q[r + 2])
                moved = jnp.where(turn, pltpu.roll(far, 1, 1), pltpu.roll(far, lanes - 1, 1))
                value = moved + jnp.where(outer, near, 0.0)
                spread[pl.ds((at + c) * rows + r, 8, stride=rows), :] = value
        at += channels
    for j in range(at // 8):
        part = spread[j * 8 * rows_a : (j + 1) * 8 * rows_a, :].astype(BF16)
        found = lax.dot_general(pick, part, dims, preferred_element_type=F32)
        stage[0, 2 * j : 2 * j + 2, :] = found[0:2, :]
        stage[1, 2 * j : 2 * j + 2, :] = found[2:4, :]
    out_a[...] = stage[0].astype(BF16)
    out_b[...] = stage[1].astype(BF16)


def remap(tile_count, block, *refs):
    table, weights, own, col_a, col_b = refs[:5]
    got = refs[5 : 4 + tile_count]
    own_out = refs[4 + tile_count]
    outs = refs[5 + tile_count : 4 + 2 * tile_count]
    band, total = refs[4 + 2 * tile_count :]
    me = lax.axis_index("tile")
    sources, targets = peers(me, tile_count)
    band[pl.ds(me * block, block)] = own[...]
    for e, ref in zip(sources, got):
        band[pl.ds(e * block, block)] = ref[...]
    total[...] = jnp.zeros_like(total)
    pairs = weights.shape[0]
    live_count = table[2, 0]
    trans = (((1,), (1,)), ((), ()))
    plain = (((1,), (0,)), ((), ()))
    group = 8
    for start in range(0, pairs, group):
        made = []
        for k in range(start, min(start + group, pairs)):
            at_a = table[0, k]
            at_o = table[1, k]
            live = k < live_count
            w = weights[k]
            ta = band[at_a]
            to = band[at_o]
            ta = jnp.where(live, ta, jnp.zeros_like(ta))
            to = jnp.where(live, to, jnp.zeros_like(to))
            ahead = lax.dot_general(ta, w, plain, preferred_element_type=F32)
            back = lax.dot_general(to, w, trans, preferred_element_type=F32)
            made.append((at_a, at_o, ahead, back))
        for at_a, at_o, ahead, back in made:
            total[at_o] += ahead
            total[at_a] += back
    own_out[...] = total[pl.ds(me * block, block)]
    lanes = weights.shape[2]
    for e, ref in zip(targets, outs):
        part = total[pl.ds(e * block, block)].astype(BF16)
        ref[0 : block * SURF, :] = part.reshape(block * SURF, lanes)
    for ref, col in zip(outs, (col_a, col_b)):
        ref[block * SURF :, :] = col[...]


def stencil(rows_a, rows_o, atm, ocean, rate, even_in, odd_in, atm_out, ocean_out):
    comp = lax.axis_index("comp")
    parity = lax.rem(comp, 2)
    lanes = atm.shape[1]
    lane = lax.broadcasted_iota(jnp.int32, (8, lanes), 1)
    at_west = lane == 0
    at_east = lane == lanes - 1
    keep_north = jnp.where(comp == 0, 0.0, 1.0).astype(F32)
    keep_south = jnp.where(comp == lax.axis_size("comp") - 1, 0.0, 1.0).astype(F32)
    at = 0
    for ref, rows, out in ((atm, rows_a, atm_out), (ocean, rows_o, ocean_out)):
        channels = ref.shape[0] // rows
        for c in range(0, channels, 8):
            rho = rate[at + c : at + c + 8, :]
            own = 1.0 - 4.0 * rho
            north, south = halo_rows(parity, even_in, odd_in, at + c)
            q = north + [ref[pl.ds(c * rows + r, 8, stride=rows), :] for r in range(rows)] + south
            p = []
            for i in range(1, rows + 3):
                west = jnp.where(at_west, 0.0, pltpu.roll(q[i], 1, 1))
                east = jnp.where(at_east, 0.0, pltpu.roll(q[i], lanes - 1, 1))
                p.append(own * q[i] + rho * ((q[i - 1] + q[i + 1]) + (west + east)))
            p[0] = p[0] * keep_north
            p[rows + 1] = p[rows + 1] * keep_south
            for r in range(rows):
                ghost = rho * q[r + 2]
                west = jnp.where(at_west, ghost, pltpu.roll(p[r + 1], 1, 1))
                east = jnp.where(at_east, ghost, pltpu.roll(p[r + 1], lanes - 1, 1))
                out[pl.ds(c * rows + r, 8, stride=rows), :] = own * p[r + 1] + rho * (
                    (p[r] + p[r + 2]) + (west + east)
                )
        at += channels


def final(tile_count, rows_a, rows_o, *refs):
    mask, atm, ocean, own = refs[:4]
    got = refs[4 : 3 + tile_count]
    atm_out, ocean_out, force, value_a, value_o, done = refs[3 + tile_count :]
    lanes = atm.shape[1]
    block = rows_a + rows_o
    message = block * SURF
    tile_parity = lax.rem(lax.axis_index("tile"), 2)
    row = lax.broadcasted_iota(jnp.int32, (8, lanes), 0)
    lane = lax.broadcasted_iota(jnp.int32, (8, lanes), 1)
    east = lax.div(row, 2) == tile_parity
    second = lax.rem(row, 2)
    spot = jnp.where(east, lanes - 1 - second, second)
    place = jnp.where((row < 4) & (lane == spot), 1.0, 0.0).astype(BF16)
    for y in range(block):
        total = own[y]
        for ref in got:
            total = total + ref[SURF * y : SURF * y + SURF, :].astype(F32)
        if y >= rows_a:
            total = total * mask[0, y - rows_a].astype(F32)
        start = y if y < rows_a else SURF * rows_a + y - rows_a
        force[pl.ds(start, SURF, stride=rows_a if y < rows_a else rows_o), :] = total
    dims = (((0,), (0,)), ((), ()))
    group = 32
    at = 0
    copies = []
    for ref, keep, out, rows, add in (
        (atm, value_a, atm_out, rows_a, 0),
        (ocean, value_o, ocean_out, rows_o, SURF * rows_a),
    ):
        channels = ref.shape[0] // rows
        for c in range(0, channels, 8):
            j = message + 2 * ((at + c) // 8)
            sides = jnp.concatenate(
                [
                    got[0][j : j + 2, :].astype(F32),
                    got[1][j : j + 2, :].astype(F32),
                    jnp.zeros((4, lanes), F32),
                ],
                axis=0,
            ).astype(BF16)
            value = ref[c * rows : (c + 8) * rows, :] + lax.dot_general(
                sides, place, dims, preferred_element_type=F32
            )
            if c == 0:
                value = value + force[add : add + SURF * rows, :]
            keep[c * rows : (c + 8) * rows, :] = value
            if (c + 8) % group == 0 or c + 8 == channels:
                begin = c // group * group * rows
                end = (c + 8) * rows
                copies.append(
                    pltpu.make_async_copy(
                        keep.at[begin:end], out.at[begin:end], done.at[len(copies)]
                    )
                )
                copies[-1].start()
        at += channels
    for copy in copies:
        copy.wait()


def params(limit=None):
    return pltpu.CompilerParams(vmem_limit_bytes=limit)


def shards(
    atm_state,
    ocean_state,
    atm_rate,
    ocean_rate,
    ocean_mask,
    remap_weight,
    pair_src,
    pair_tgt,
    pair_count,
):
    channels_a, rows_a, lanes = atm_state.shape
    channels_o, rows_o, _ = ocean_state.shape
    channels = channels_a + channels_o
    tile_count = lax.axis_size("tile")
    block = rows_a + rows_o
    message = block * SURF
    extra = -(-2 * channels // 8 // 16) * 16
    atm = atm_state.reshape(channels_a * rows_a, lanes)
    ocean = ocean_state.reshape(channels_o * rows_o, lanes)
    mask = ocean_mask.reshape(1, rows_o)
    routes = tile_pairs(tile_count)
    even_pairs, odd_pairs = comp_pairs(lax.axis_size("comp"))

    surface = pl.pallas_call(
        functools.partial(pack_surface, rows_a, rows_o),
        in_specs=[HBM] * 3,
        out_specs=VMEM,
        out_shape=jax.ShapeDtypeStruct((block, SURF, lanes), BF16),
        scratch_shapes=[
            pltpu.SMEM((1, rows_o), jnp.int32),
            pltpu.VMEM((SURF * rows_a, lanes), F32),
            pltpu.VMEM((SURF * rows_o, lanes), F32),
            pltpu.SemaphoreType.DMA((3,)),
        ],
        compiler_params=params(4 << 20),
        name="pack_surface",
    )(mask, atm, ocean)
    received = [lax.ppermute(surface, "tile", route) for route in routes]

    halo = jax.ShapeDtypeStruct((2, channels, lanes), BF16)
    even_rows, odd_rows, table, rate = pl.pallas_call(
        functools.partial(prepare, rows_a, rows_o),
        in_specs=[ANY] + [VMEM] * 7,
        out_specs=[VMEM] * 4,
        out_shape=[
            halo,
            halo,
            jax.ShapeDtypeStruct((8, lanes), jnp.int32),
            jax.ShapeDtypeStruct((channels, lanes), F32),
        ],
        compiler_params=params(8 << 20),
        name="prepare",
    )(
        surface,
        atm,
        ocean,
        atm_rate.reshape(1, channels_a),
        ocean_rate.reshape(1, channels_o),
        pair_src,
        pair_tgt,
        pair_count,
    )
    even_in = lax.ppermute(even_rows, "comp", even_pairs)
    odd_in = lax.ppermute(odd_rows, "comp", odd_pairs)

    col_a, col_b = pl.pallas_call(
        functools.partial(pack_columns, rows_a, rows_o),
        in_specs=[VMEM] * 5,
        out_specs=[VMEM, VMEM],
        out_shape=[jax.ShapeDtypeStruct((extra, lanes), BF16)] * 2,
        scratch_shapes=[
            pltpu.VMEM((channels_a * rows_a + channels_o * rows_o, lanes), F32),
            pltpu.VMEM((2, extra, lanes), F32),
        ],
        compiler_params=params(8 << 20),
        name="pack_columns",
    )(atm, ocean, rate, even_in, odd_in)

    sends = [jax.ShapeDtypeStruct((message + extra, lanes), BF16)] * 2
    sends += [jax.ShapeDtypeStruct((message, lanes), BF16)] * (tile_count - 3)
    own_part, *parts = pl.pallas_call(
        functools.partial(remap, tile_count, block),
        in_specs=[SMEM] + [VMEM] * (3 + tile_count),
        out_specs=[VMEM] * tile_count,
        out_shape=[jax.ShapeDtypeStruct((block, SURF, lanes), F32)] + sends,
        scratch_shapes=[
            pltpu.VMEM((tile_count * block, SURF, lanes), BF16),
            pltpu.VMEM((tile_count * block, SURF, lanes), F32),
        ],
        compiler_params=params(12 << 20),
        name="remap",
    )(table, remap_weight[0], surface, col_a, col_b, *received)
    returned = [lax.ppermute(part, "tile", route) for part, route in zip(parts, routes)]

    atm_base, ocean_base = pl.pallas_call(
        functools.partial(stencil, rows_a, rows_o),
        in_specs=[VMEM] * 5,
        out_specs=[VMEM, VMEM],
        out_shape=[
            jax.ShapeDtypeStruct(atm.shape, F32),
            jax.ShapeDtypeStruct(ocean.shape, F32),
        ],
        compiler_params=params(8 << 20),
        name="stencil",
    )(atm, ocean, rate, even_in, odd_in)

    atm_next, ocean_next = pl.pallas_call(
        functools.partial(final, tile_count, rows_a, rows_o),
        in_specs=[SMEM] + [VMEM] * (2 + tile_count),
        out_specs=[HBM, HBM],
        out_shape=[
            jax.ShapeDtypeStruct(atm.shape, F32),
            jax.ShapeDtypeStruct(ocean.shape, F32),
        ],
        scratch_shapes=[
            pltpu.VMEM((SURF * block, lanes), F32),
            pltpu.VMEM(atm.shape, F32),
            pltpu.VMEM(ocean.shape, F32),
            pltpu.SemaphoreType.DMA((channels // 8,)),
        ],
        compiler_params=params(12 << 20),
        name="final",
    )(mask, atm_base, ocean_base, own_part, *returned)
    return (
        atm_next.reshape(channels_a, rows_a, lanes),
        ocean_next.reshape(channels_o, rows_o, lanes),
    )


def solution(mesh):
    return jax.shard_map(
        shards,
        mesh=mesh,
        in_specs=(
            P(None, "comp", "tile"),
            P(None, "comp", "tile"),
            P(),
            P(),
            P("comp", "tile"),
            P("comp", "tile", None, None),
            P("comp", "tile"),
            P("comp", "tile"),
            P("comp", "tile"),
        ),
        out_specs=(P(None, "comp", "tile"), P(None, "comp", "tile")),
        check_vma=False,
    )
```

```python
import functools

import jax
import jax.numpy as jnp
from jax import lax
from jax.experimental import pallas as pl
from jax.experimental.pallas import tpu as pltpu
from jax.sharding import PartitionSpec as P


SURF = 8
F32 = jnp.float32
BF16 = jnp.bfloat16
VMEM = pl.BlockSpec(memory_space=pltpu.VMEM)
SMEM = pl.BlockSpec(memory_space=pltpu.SMEM)
HBM = pl.BlockSpec(memory_space=pltpu.HBM)
ANY = pl.BlockSpec(memory_space=pl.ANY)


def beside_even(index):
    return index + 1 - 2 * (index % 2)


def beside_odd(index, count):
    return (index - 1 + 2 * (index % 2) + count) % count


def tile_pairs(count):
    routes = [
        [(i, beside_even(i)) for i in range(count)],
        [(i, beside_odd(i, count)) for i in range(count)],
    ]
    routes += [[(i, (i + s) % count) for i in range(count)] for s in range(2, count - 1)]
    return routes


def peers(me, count):
    a = beside_even(me)
    b = beside_odd(me, count)
    far = range(2, count - 1)
    sources = [a, b] + [lax.rem(me - s + count, count) for s in far]
    targets = [a, b] + [lax.rem(me + s, count) for s in far]
    return sources, targets


def comp_pairs(count):
    even = [(i, beside_even(i)) for i in range(count)]
    odd = [(i, i + 1) for i in range(1, count - 1, 2)] + [(i + 1, i) for i in range(1, count - 1, 2)]
    return even, odd


def prepare(rows_a, rows_o, *refs):
    ins, outs = refs[:7], refs[7:15]
    rate_a, rate_o, done = refs[15:]
    atm_in, ocean_in, mask_in, src_in, tgt_in, rate_a_in, rate_o_in = ins
    atm, ocean, surface, even_out, odd_out, rate, table, mask = outs
    copies = [
        (mask_in, mask),
        (atm_in.at[0 : SURF * rows_a], atm.at[0 : SURF * rows_a]),
        (ocean_in.at[0 : SURF * rows_o], ocean.at[0 : SURF * rows_o]),
        (src_in, table.at[0:1]),
        (tgt_in, table.at[1:2]),
        (rate_a_in, rate_a),
        (rate_o_in, rate_o),
        (atm_in.at[SURF * rows_a :], atm.at[SURF * rows_a :]),
        (ocean_in.at[SURF * rows_o :], ocean.at[SURF * rows_o :]),
    ]
    copies = [pltpu.make_async_copy(a, b, done.at[i]) for i, (a, b) in enumerate(copies)]
    for copy in copies:
        copy.start()
    copies[1].wait()
    for y in range(rows_a):
        surface[y] = atm[pl.ds(y, SURF, stride=rows_a), :].astype(BF16)
    copies[0].wait()
    copies[2].wait()
    for y in range(rows_o):
        tile = ocean[pl.ds(y, SURF, stride=rows_o), :]
        surface[rows_a + y] = (tile * mask[0, y].astype(F32)).astype(BF16)
    for copy in copies[3:]:
        copy.wait()
    lanes = atm.shape[1]
    split = rate_a.shape[1]
    rate[0:split, :] = jnp.broadcast_to(rate_a[...], (lanes, split)).T
    rate[split:, :] = jnp.broadcast_to(rate_o[...], (lanes, rate_o.shape[1])).T
    parity = lax.rem(lax.axis_index("comp"), 2)
    at = 0
    for ref, rows in ((atm, rows_a), (ocean, rows_o)):
        channels = ref.shape[0] // rows
        for c in range(0, channels, 8):
            for r in range(2):
                low = ref[pl.ds(c * rows + r, 8, stride=rows), :]
                high = ref[pl.ds(c * rows + rows - 2 + r, 8, stride=rows), :]
                even_out[r, at + c : at + c + 8, :] = jnp.where(parity == 0, high, low).astype(BF16)
                odd_out[r, at + c : at + c + 8, :] = jnp.where(parity == 0, low, high).astype(BF16)
        at += channels


def halo_rows(parity, even_in, odd_in, at):
    e = [even_in[r, at : at + 8, :].astype(F32) for r in range(2)]
    o = [odd_in[r, at : at + 8, :].astype(F32) for r in range(2)]
    north = [jnp.where(parity == 0, o[r], e[r]) for r in range(2)]
    south = [jnp.where(parity == 0, e[r], o[r]) for r in range(2)]
    return north, south


def pack_columns(rows_a, rows_o, atm, ocean, rate, even_in, odd_in, out_a, out_b, spread, stage):
    parity = lax.rem(lax.axis_index("comp"), 2)
    tile_parity = lax.rem(lax.axis_index("tile"), 2)
    lanes = atm.shape[1]
    row = lax.broadcasted_iota(jnp.int32, (8, lanes), 0)
    lane = lax.broadcasted_iota(jnp.int32, (8, lanes), 1)
    east = lax.div(row, 2) == tile_parity
    second = lax.rem(row, 2)
    spot = jnp.where(east, lanes - 1 - second, second)
    pick = jnp.where((row < 4) & (lane == spot), 1.0, 0.0).astype(BF16)
    outer = (lane == 0) | (lane == lanes - 1)
    turn = (lane == 1) | (lane == lanes - 1)
    dims = (((1,), (1,)), ((), ()))
    stage[...] = jnp.zeros_like(stage)
    at = 0
    for ref, rows in ((atm, rows_a), (ocean, rows_o)):
        channels = ref.shape[0] // rows
        for c in range(0, channels, 8):
            rho = rate[at + c : at + c + 8, :]
            own = 2.0 * rho * (1.0 - 4.0 * rho)
            square = rho * rho
            north, south = halo_rows(parity, even_in, odd_in, at + c)
            q = [north[1]]
            q += [ref[pl.ds(c * rows + r, 8, stride=rows), :] for r in range(rows)]
            q += [south[0]]
            for r in range(rows):
                far = square * q[r + 1]
                near = own * q[r + 1] + 2.0 * square * (q[r] + q[r + 2])
                moved = jnp.where(turn, pltpu.roll(far, 1, 1), pltpu.roll(far, lanes - 1, 1))
                value = moved + jnp.where(outer, near, 0.0)
                spread[pl.ds((at + c) * rows + r, 8, stride=rows), :] = value
        at += channels
    for j in range(at // 8):
        part = spread[j * 8 * rows_a : (j + 1) * 8 * rows_a, :].astype(BF16)
        found = lax.dot_general(pick, part, dims, preferred_element_type=F32)
        stage[0, 2 * j : 2 * j + 2, :] = found[0:2, :]
        stage[1, 2 * j : 2 * j + 2, :] = found[2:4, :]
    out_a[...] = stage[0].astype(BF16)
    out_b[...] = stage[1].astype(BF16)


def remap(tile_count, rows_a, rows_o, *refs):
    table, number, weights, own, col_a, col_b = refs[:6]
    got = refs[6 : 5 + tile_count]
    own_out = refs[5 + tile_count]
    outs = refs[6 + tile_count : 5 + 2 * tile_count]
    band, total = refs[5 + 2 * tile_count :]
    block = rows_a + rows_o
    me = lax.axis_index("tile")
    sources, targets = peers(me, tile_count)
    band[pl.ds(me * block, block)] = own[...]
    for e, ref in zip(sources, got):
        band[pl.ds(e * block, block)] = ref[...]
    total[...] = jnp.zeros_like(total)
    pairs = weights.shape[0]
    live_count = number[0, 0]
    trans = (((1,), (1,)), ((), ()))
    plain = (((1,), (0,)), ((), ()))
    group = 8
    for start in range(0, pairs, group):
        made = []
        for k in range(start, min(start + group, pairs)):
            a = table[0, k]
            o = table[1, k]
            at_a = lax.div(a, rows_a) * block + lax.rem(a, rows_a)
            at_o = lax.div(o, rows_o) * block + rows_a + lax.rem(o, rows_o)
            live = k < live_count
            w = weights[k]
            ta = band[at_a]
            to = band[at_o]
            ta = jnp.where(live, ta, jnp.zeros_like(ta))
            to = jnp.where(live, to, jnp.zeros_like(to))
            ahead = lax.dot_general(ta, w, plain, preferred_element_type=F32)
            back = lax.dot_general(to, w, trans, preferred_element_type=F32)
            made.append((at_a, at_o, ahead, back))
        for at_a, at_o, ahead, back in made:
            total[at_o] += ahead
            total[at_a] += back
    own_out[...] = total[pl.ds(me * block, block)]
    lanes = weights.shape[2]
    for e, ref in zip(targets, outs):
        part = total[pl.ds(e * block, block)].astype(BF16)
        ref[0 : block * SURF, :] = part.reshape(block * SURF, lanes)
    for ref, col in zip(outs, (col_a, col_b)):
        ref[block * SURF :, :] = col[...]


def stencil(rows_a, rows_o, atm, ocean, rate, even_in, odd_in, atm_out, ocean_out):
    comp = lax.axis_index("comp")
    parity = lax.rem(comp, 2)
    lanes = atm.shape[1]
    lane = lax.broadcasted_iota(jnp.int32, (8, lanes), 1)
    at_west = lane == 0
    at_east = lane == lanes - 1
    keep_north = jnp.where(comp == 0, 0.0, 1.0).astype(F32)
    keep_south = jnp.where(comp == lax.axis_size("comp") - 1, 0.0, 1.0).astype(F32)
    at = 0
    for ref, rows, out in ((atm, rows_a, atm_out), (ocean, rows_o, ocean_out)):
        channels = ref.shape[0] // rows
        for c in range(0, channels, 8):
            rho = rate[at + c : at + c + 8, :]
            own = 1.0 - 4.0 * rho
            north, south = halo_rows(parity, even_in, odd_in, at + c)
            q = north + [ref[pl.ds(c * rows + r, 8, stride=rows), :] for r in range(rows)] + south
            p = []
            for i in range(1, rows + 3):
                west = jnp.where(at_west, 0.0, pltpu.roll(q[i], 1, 1))
                east = jnp.where(at_east, 0.0, pltpu.roll(q[i], lanes - 1, 1))
                p.append(own * q[i] + rho * ((q[i - 1] + q[i + 1]) + (west + east)))
            p[0] = p[0] * keep_north
            p[rows + 1] = p[rows + 1] * keep_south
            for r in range(rows):
                ghost = rho * q[r + 2]
                west = jnp.where(at_west, ghost, pltpu.roll(p[r + 1], 1, 1))
                east = jnp.where(at_east, ghost, pltpu.roll(p[r + 1], lanes - 1, 1))
                out[pl.ds(c * rows + r, 8, stride=rows), :] = own * p[r + 1] + rho * (
                    (p[r] + p[r + 2]) + (west + east)
                )
        at += channels


def final(tile_count, rows_a, rows_o, *refs):
    mask, atm, ocean, own = refs[:4]
    got = refs[4 : 3 + tile_count]
    atm_out, ocean_out, force, value_a, value_o, done = refs[3 + tile_count :]
    lanes = atm.shape[1]
    block = rows_a + rows_o
    message = block * SURF
    tile_parity = lax.rem(lax.axis_index("tile"), 2)
    row = lax.broadcasted_iota(jnp.int32, (8, lanes), 0)
    lane = lax.broadcasted_iota(jnp.int32, (8, lanes), 1)
    east = lax.div(row, 2) == tile_parity
    second = lax.rem(row, 2)
    spot = jnp.where(east, lanes - 1 - second, second)
    place = jnp.where((row < 4) & (lane == spot), 1.0, 0.0).astype(BF16)
    for y in range(block):
        total = own[y]
        for ref in got:
            total = total + ref[SURF * y : SURF * y + SURF, :].astype(F32)
        if y >= rows_a:
            total = total * mask[0, y - rows_a].astype(F32)
        start = y if y < rows_a else SURF * rows_a + y - rows_a
        force[pl.ds(start, SURF, stride=rows_a if y < rows_a else rows_o), :] = total
    dims = (((0,), (0,)), ((), ()))
    group = 32
    at = 0
    copies = []
    for ref, keep, out, rows, add in (
        (atm, value_a, atm_out, rows_a, 0),
        (ocean, value_o, ocean_out, rows_o, SURF * rows_a),
    ):
        channels = ref.shape[0] // rows
        for c in range(0, channels, 8):
            j = message + 2 * ((at + c) // 8)
            sides = jnp.concatenate(
                [
                    got[0][j : j + 2, :].astype(F32),
                    got[1][j : j + 2, :].astype(F32),
                    jnp.zeros((4, lanes), F32),
                ],
                axis=0,
            ).astype(BF16)
            value = ref[c * rows : (c + 8) * rows, :] + lax.dot_general(
                sides, place, dims, preferred_element_type=F32
            )
            if c == 0:
                value = value + force[add : add + SURF * rows, :]
            keep[c * rows : (c + 8) * rows, :] = value
            if (c + 8) % group == 0 or c + 8 == channels:
                begin = c // group * group * rows
                end = (c + 8) * rows
                copies.append(
                    pltpu.make_async_copy(
                        keep.at[begin:end], out.at[begin:end], done.at[len(copies)]
                    )
                )
                copies[-1].start()
        at += channels
    for copy in copies:
        copy.wait()


def call(body, micros, limit, **rest):
    return pl.pallas_call(
        body,
        compiler_params=pltpu.CompilerParams(vmem_limit_bytes=limit),
        cost_estimate=pl.CostEstimate(
            flops=0, transcendentals=0, bytes_accessed=int(micros * 3.0e6)
        ),
        **rest,
    )


def exchange(blocks, routes):
    out = []
    for block, route in zip(blocks, routes):
        out.append(lax.ppermute(block, "tile", route))
    return out


def interval(
    atm_state,
    ocean_state,
    atm_rate,
    ocean_rate,
    ocean_mask,
    remap_weight,
    pair_src,
    pair_tgt,
    pair_count,
):
    channels_a, rows_a, lanes = atm_state.shape
    channels_o, rows_o, _ = ocean_state.shape
    channels = channels_a + channels_o
    tile_count = lax.axis_size("tile")
    block = rows_a + rows_o
    message = block * SURF
    extra = -(-2 * channels // 8 // 16) * 16
    atm = atm_state.reshape(channels_a * rows_a, lanes)
    ocean = ocean_state.reshape(channels_o * rows_o, lanes)
    mask = ocean_mask.reshape(1, rows_o)
    routes = tile_pairs(tile_count)
    even_pairs, odd_pairs = comp_pairs(lax.axis_size("comp"))

    halo = pltpu.VMEM((2, channels, lanes), BF16)
    atm, ocean, surface, even_rows, odd_rows, rate, table, mask = call(
        functools.partial(prepare, rows_a, rows_o),
        1.5,
        8 << 20,
        in_specs=[HBM] * 7,
        out_specs=[VMEM] * 6 + [SMEM] * 2,
        out_shape=[
            pltpu.VMEM(atm.shape, F32),
            pltpu.VMEM(ocean.shape, F32),
            pltpu.VMEM((block, SURF, lanes), BF16),
            halo,
            halo,
            pltpu.VMEM((channels, lanes), F32),
            pltpu.SMEM((2, pair_src.shape[1]), jnp.int32),
            pltpu.SMEM((1, rows_o), jnp.int32),
        ],
        scratch_shapes=[
            pltpu.VMEM((1, channels_a), F32),
            pltpu.VMEM((1, channels_o), F32),
            pltpu.SemaphoreType.DMA((9,)),
        ],
        name="prepare",
    )(
        *[
            pltpu.with_memory_space_constraint(x, pltpu.HBM)
            for x in (
                atm,
                ocean,
                mask,
                pair_src,
                pair_tgt,
                atm_rate.reshape(1, channels_a),
                ocean_rate.reshape(1, channels_o),
            )
        ]
    )
    received = exchange([surface] * len(routes), routes)

    even_in = lax.ppermute(even_rows, "comp", even_pairs)
    odd_in = lax.ppermute(odd_rows, "comp", odd_pairs)

    col_a, col_b = call(
        functools.partial(pack_columns, rows_a, rows_o),
        1.2,
        8 << 20,
        in_specs=[VMEM] * 5,
        out_specs=[VMEM, VMEM],
        out_shape=[jax.ShapeDtypeStruct((extra, lanes), BF16)] * 2,
        scratch_shapes=[
            pltpu.VMEM((channels_a * rows_a + channels_o * rows_o, lanes), F32),
            pltpu.VMEM((2, extra, lanes), F32),
        ],
        name="pack_columns",
    )(atm, ocean, rate, even_in, odd_in)

    sends = [jax.ShapeDtypeStruct((message + extra, lanes), BF16)] * 2
    sends += [jax.ShapeDtypeStruct((message, lanes), BF16)] * (tile_count - 3)
    own_part, *parts = call(
        functools.partial(remap, tile_count, rows_a, rows_o),
        2.0,
        12 << 20,
        in_specs=[SMEM, SMEM] + [VMEM] * (3 + tile_count),
        out_specs=[VMEM] * tile_count,
        out_shape=[jax.ShapeDtypeStruct((block, SURF, lanes), F32)] + sends,
        scratch_shapes=[
            pltpu.VMEM((tile_count * block, SURF, lanes), BF16),
            pltpu.VMEM((tile_count * block, SURF, lanes), F32),
        ],
        name="remap",
    )(table, pair_count, remap_weight[0], surface, col_a, col_b, *received)
    returned = exchange(parts, routes)

    atm_base, ocean_base = call(
        functools.partial(stencil, rows_a, rows_o),
        2.5,
        8 << 20,
        in_specs=[VMEM] * 5,
        out_specs=[VMEM, VMEM],
        out_shape=[
            jax.ShapeDtypeStruct(atm.shape, F32),
            jax.ShapeDtypeStruct(ocean.shape, F32),
        ],
        name="stencil",
    )(atm, ocean, rate, even_in, odd_in)

    atm_next, ocean_next = call(
        functools.partial(final, tile_count, rows_a, rows_o),
        2.0,
        12 << 20,
        in_specs=[SMEM] + [VMEM] * (2 + tile_count),
        out_specs=[HBM, HBM],
        out_shape=[
            jax.ShapeDtypeStruct(atm.shape, F32),
            jax.ShapeDtypeStruct(ocean.shape, F32),
        ],
        scratch_shapes=[
            pltpu.VMEM((SURF * block, lanes), F32),
            pltpu.VMEM(atm.shape, F32),
            pltpu.VMEM(ocean.shape, F32),
            pltpu.SemaphoreType.DMA((channels // 8,)),
        ],
        name="final",
    )(mask, atm_base, ocean_base, own_part, *returned)
    return (
        atm_next.reshape(channels_a, rows_a, lanes),
        ocean_next.reshape(channels_o, rows_o, lanes),
    )


def solution(mesh):
    return jax.shard_map(
        interval,
        mesh=mesh,
        in_specs=(
            P(None, "comp", "tile"),
            P(None, "comp", "tile"),
            P(),
            P(),
            P("comp", "tile"),
            P("comp", "tile", None, None),
            P("comp", "tile"),
            P("comp", "tile"),
            P("comp", "tile"),
        ),
        out_specs=(P(None, "comp", "tile"), P(None, "comp", "tile")),
        check_vma=False,
    )
```

```python
import functools

import jax
import jax.numpy as jnp
from jax import lax
from jax.experimental import pallas as pl
from jax.experimental.pallas import tpu as pltpu
from jax.sharding import PartitionSpec as P


SURF = 8
F32 = jnp.float32
BF16 = jnp.bfloat16
VMEM = pl.BlockSpec(memory_space=pltpu.VMEM)
SMEM = pl.BlockSpec(memory_space=pltpu.SMEM)
HBM = pl.BlockSpec(memory_space=pltpu.HBM)
ANY = pl.BlockSpec(memory_space=pl.ANY)


def beside_even(index):
    return index + 1 - 2 * (index % 2)


def beside_odd(index, count):
    return (index - 1 + 2 * (index % 2) + count) % count


def tile_pairs(count):
    routes = [
        [(i, beside_even(i)) for i in range(count)],
        [(i, beside_odd(i, count)) for i in range(count)],
    ]
    routes += [[(i, (i + s) % count) for i in range(count)] for s in range(2, count - 1)]
    return routes


def peers(me, count):
    a = beside_even(me)
    b = beside_odd(me, count)
    far = range(2, count - 1)
    sources = [a, b] + [lax.rem(me - s + count, count) for s in far]
    targets = [a, b] + [lax.rem(me + s, count) for s in far]
    return sources, targets


def comp_pairs(count):
    even = [(i, beside_even(i)) for i in range(count)]
    odd = [(i, i + 1) for i in range(1, count - 1, 2)] + [(i + 1, i) for i in range(1, count - 1, 2)]
    return even, odd


def pack_surface(rows_a, rows_o, atm_in, ocean_in, mask_in, surface, mask, atm, ocean, done):
    copies = [
        (mask_in, mask),
        (atm_in.at[0 : SURF * rows_a], atm),
        (ocean_in.at[0 : SURF * rows_o], ocean),
    ]
    copies = [pltpu.make_async_copy(a, b, done.at[i]) for i, (a, b) in enumerate(copies)]
    for copy in copies:
        copy.start()
    copies[1].wait()
    for y in range(rows_a):
        surface[y] = atm[pl.ds(y, SURF, stride=rows_a), :].astype(BF16)
    copies[0].wait()
    copies[2].wait()
    for y in range(rows_o):
        tile = ocean[pl.ds(y, SURF, stride=rows_o), :]
        surface[rows_a + y] = (tile * mask[0, y].astype(F32)).astype(BF16)


def prepare(rows_a, rows_o, *refs):
    atm_in, ocean_in, number, src_in, tgt_in, rate_a_in, rate_o_in = refs[:7]
    atm, ocean, even_out, odd_out, rate, table, live, rate_a, rate_o, done = refs[7:]
    live[0, 0] = number[0, 0]
    copies = [
        (atm_in, atm),
        (ocean_in, ocean),
        (rate_a_in, rate_a),
        (rate_o_in, rate_o),
        (src_in, table.at[0:1]),
        (tgt_in, table.at[1:2]),
    ]
    copies = [pltpu.make_async_copy(a, b, done.at[i]) for i, (a, b) in enumerate(copies)]
    for copy in copies:
        copy.start()
    for copy in copies[2:]:
        copy.wait()
    lanes = atm.shape[1]
    split = rate_a.shape[1]
    rate[0:split, :] = jnp.broadcast_to(rate_a[...], (lanes, split)).T
    rate[split:, :] = jnp.broadcast_to(rate_o[...], (lanes, rate_o.shape[1])).T
    parity = lax.rem(lax.axis_index("comp"), 2)
    at = 0
    for copy, ref, rows in ((copies[0], atm, rows_a), (copies[1], ocean, rows_o)):
        copy.wait()
        channels = ref.shape[0] // rows
        for c in range(0, channels, 8):
            for r in range(2):
                low = ref[pl.ds(c * rows + r, 8, stride=rows), :]
                high = ref[pl.ds(c * rows + rows - 2 + r, 8, stride=rows), :]
                even_out[r, at + c : at + c + 8, :] = jnp.where(parity == 0, high, low).astype(BF16)
                odd_out[r, at + c : at + c + 8, :] = jnp.where(parity == 0, low, high).astype(BF16)
        at += channels


def halo_rows(parity, even_in, odd_in, at):
    e = [even_in[r, at : at + 8, :].astype(F32) for r in range(2)]
    o = [odd_in[r, at : at + 8, :].astype(F32) for r in range(2)]
    north = [jnp.where(parity == 0, o[r], e[r]) for r in range(2)]
    south = [jnp.where(parity == 0, e[r], o[r]) for r in range(2)]
    return north, south


def pack_columns(rows_a, rows_o, atm, ocean, rate, even_in, odd_in, part_a, part_b, out_a, out_b, spread, stage):
    del part_a, part_b
    parity = lax.rem(lax.axis_index("comp"), 2)
    tile_parity = lax.rem(lax.axis_index("tile"), 2)
    lanes = atm.shape[1]
    row = lax.broadcasted_iota(jnp.int32, (8, lanes), 0)
    lane = lax.broadcasted_iota(jnp.int32, (8, lanes), 1)
    east = lax.div(row, 2) == tile_parity
    second = lax.rem(row, 2)
    spot = jnp.where(east, lanes - 1 - second, second)
    pick = jnp.where((row < 4) & (lane == spot), 1.0, 0.0).astype(BF16)
    outer = (lane == 0) | (lane == lanes - 1)
    turn = (lane == 1) | (lane == lanes - 1)
    dims = (((1,), (1,)), ((), ()))
    stage[...] = jnp.zeros_like(stage)
    at = 0
    for ref, rows in ((atm, rows_a), (ocean, rows_o)):
        channels = ref.shape[0] // rows
        for c in range(0, channels, 8):
            rho = rate[at + c : at + c + 8, :]
            own = 2.0 * rho * (1.0 - 4.0 * rho)
            square = rho * rho
            north, south = halo_rows(parity, even_in, odd_in, at + c)
            q = [north[1]]
            q += [ref[pl.ds(c * rows + r, 8, stride=rows), :] for r in range(rows)]
            q += [south[0]]
            for r in range(rows):
                far = square * q[r + 1]
                near = own * q[r + 1] + 2.0 * square * (q[r] + q[r + 2])
                moved = jnp.where(turn, pltpu.roll(far, 1, 1), pltpu.roll(far, lanes - 1, 1))
                value = moved + jnp.where(outer, near, 0.0)
                spread[pl.ds((at + c) * rows + r, 8, stride=rows), :] = value
        at += channels
    for j in range(at // 8):
        part = spread[j * 8 * rows_a : (j + 1) * 8 * rows_a, :].astype(BF16)
        found = lax.dot_general(pick, part, dims, preferred_element_type=F32)
        stage[0, 2 * j : 2 * j + 2, :] = found[0:2, :]
        stage[1, 2 * j : 2 * j + 2, :] = found[2:4, :]
    behind = out_a.shape[0] - stage.shape[1]
    out_a[behind:, :] = stage[0].astype(BF16)
    out_b[behind:, :] = stage[1].astype(BF16)


def remap(tile_count, rows_a, rows_o, *refs):
    table, number, weights, own = refs[:4]
    got = refs[4 : 3 + tile_count]
    own_out = refs[3 + tile_count]
    outs = refs[4 + tile_count : 3 + 2 * tile_count]
    band, total = refs[3 + 2 * tile_count :]
    block = rows_a + rows_o
    me = lax.axis_index("tile")
    sources, targets = peers(me, tile_count)
    band[pl.ds(me * block, block)] = own[...]
    for e, ref in zip(sources, got):
        band[pl.ds(e * block, block)] = ref[...]
    total[...] = jnp.zeros_like(total)
    pairs = weights.shape[0]
    live_count = number[0, 0]
    trans = (((1,), (1,)), ((), ()))
    plain = (((1,), (0,)), ((), ()))
    group = 8
    for start in range(0, pairs, group):
        made = []
        for k in range(start, min(start + group, pairs)):
            a = table[0, k]
            o = table[1, k]
            at_a = lax.div(a, rows_a) * block + lax.rem(a, rows_a)
            at_o = lax.div(o, rows_o) * block + rows_a + lax.rem(o, rows_o)
            live = k < live_count
            w = weights[k]
            ta = band[at_a]
            to = band[at_o]
            ta = jnp.where(live, ta, jnp.zeros_like(ta))
            to = jnp.where(live, to, jnp.zeros_like(to))
            ahead = lax.dot_general(ta, w, plain, preferred_element_type=F32)
            back = lax.dot_general(to, w, trans, preferred_element_type=F32)
            made.append((at_a, at_o, ahead, back))
        for at_a, at_o, ahead, back in made:
            total[at_o] += ahead
            total[at_a] += back
    own_out[...] = total[pl.ds(me * block, block)]
    lanes = weights.shape[2]
    for e, ref in zip(targets, outs):
        part = total[pl.ds(e * block, block)].astype(BF16)
        ref[0 : block * SURF, :] = part.reshape(block * SURF, lanes)


def stencil(rows_a, rows_o, atm, ocean, rate, even_in, odd_in, atm_out, ocean_out):
    comp = lax.axis_index("comp")
    parity = lax.rem(comp, 2)
    lanes = atm.shape[1]
    lane = lax.broadcasted_iota(jnp.int32, (8, lanes), 1)
    at_west = lane == 0
    at_east = lane == lanes - 1
    keep_north = jnp.where(comp == 0, 0.0, 1.0).astype(F32)
    keep_south = jnp.where(comp == lax.axis_size("comp") - 1, 0.0, 1.0).astype(F32)
    at = 0
    for ref, rows, out in ((atm, rows_a, atm_out), (ocean, rows_o, ocean_out)):
        channels = ref.shape[0] // rows
        for c in range(0, channels, 8):
            rho = rate[at + c : at + c + 8, :]
            own = 1.0 - 4.0 * rho
            north, south = halo_rows(parity, even_in, odd_in, at + c)
            q = north + [ref[pl.ds(c * rows + r, 8, stride=rows), :] for r in range(rows)] + south
            p = []
            for i in range(1, rows + 3):
                west = jnp.where(at_west, 0.0, pltpu.roll(q[i], 1, 1))
                east = jnp.where(at_east, 0.0, pltpu.roll(q[i], lanes - 1, 1))
                p.append(own * q[i] + rho * ((q[i - 1] + q[i + 1]) + (west + east)))
            p[0] = p[0] * keep_north
            p[rows + 1] = p[rows + 1] * keep_south
            for r in range(rows):
                ghost = rho * q[r + 2]
                west = jnp.where(at_west, ghost, pltpu.roll(p[r + 1], 1, 1))
                east = jnp.where(at_east, ghost, pltpu.roll(p[r + 1], lanes - 1, 1))
                out[pl.ds(c * rows + r, 8, stride=rows), :] = own * p[r + 1] + rho * (
                    (p[r] + p[r + 2]) + (west + east)
                )
        at += channels


def final(tile_count, rows_a, rows_o, *refs):
    mask, atm, ocean, own = refs[:4]
    got = refs[4 : 3 + tile_count]
    atm_out, ocean_out, force, value_a, value_o, done = refs[3 + tile_count :]
    lanes = atm.shape[1]
    block = rows_a + rows_o
    message = block * SURF
    tile_parity = lax.rem(lax.axis_index("tile"), 2)
    row = lax.broadcasted_iota(jnp.int32, (8, lanes), 0)
    lane = lax.broadcasted_iota(jnp.int32, (8, lanes), 1)
    east = lax.div(row, 2) == tile_parity
    second = lax.rem(row, 2)
    spot = jnp.where(east, lanes - 1 - second, second)
    place = jnp.where((row < 4) & (lane == spot), 1.0, 0.0).astype(BF16)
    for y in range(block):
        total = own[y]
        for ref in got:
            total = total + ref[SURF * y : SURF * y + SURF, :].astype(F32)
        if y >= rows_a:
            total = total * mask[0, y - rows_a].astype(F32)
        start = y if y < rows_a else SURF * rows_a + y - rows_a
        force[pl.ds(start, SURF, stride=rows_a if y < rows_a else rows_o), :] = total
    dims = (((0,), (0,)), ((), ()))
    group = 32
    at = 0
    copies = []
    for ref, keep, out, rows, add in (
        (atm, value_a, atm_out, rows_a, 0),
        (ocean, value_o, ocean_out, rows_o, SURF * rows_a),
    ):
        channels = ref.shape[0] // rows
        for c in range(0, channels, 8):
            j = message + 2 * ((at + c) // 8)
            sides = jnp.concatenate(
                [
                    got[0][j : j + 2, :].astype(F32),
                    got[1][j : j + 2, :].astype(F32),
                    jnp.zeros((4, lanes), F32),
                ],
                axis=0,
            ).astype(BF16)
            value = ref[c * rows : (c + 8) * rows, :] + lax.dot_general(
                sides, place, dims, preferred_element_type=F32
            )
            if c == 0:
                value = value + force[add : add + SURF * rows, :]
            keep[c * rows : (c + 8) * rows, :] = value
            if (c + 8) % group == 0 or c + 8 == channels:
                begin = c // group * group * rows
                end = (c + 8) * rows
                copies.append(
                    pltpu.make_async_copy(
                        keep.at[begin:end], out.at[begin:end], done.at[len(copies)]
                    )
                )
                copies[-1].start()
        at += channels
    for copy in copies:
        copy.wait()


def call(body, micros, limit, **rest):
    return pl.pallas_call(
        body,
        compiler_params=pltpu.CompilerParams(vmem_limit_bytes=limit),
        cost_estimate=pl.CostEstimate(
            flops=0, transcendentals=0, bytes_accessed=int(micros * 3.0e6)
        ),
        **rest,
    )


def exchange(blocks, routes):
    out = []
    for block, route in zip(blocks, routes):
        out.append(lax.ppermute(block, "tile", route))
    return out


def interval(
    atm_state,
    ocean_state,
    atm_rate,
    ocean_rate,
    ocean_mask,
    remap_weight,
    pair_src,
    pair_tgt,
    pair_count,
):
    channels_a, rows_a, lanes = atm_state.shape
    channels_o, rows_o, _ = ocean_state.shape
    channels = channels_a + channels_o
    tile_count = lax.axis_size("tile")
    block = rows_a + rows_o
    message = block * SURF
    extra = -(-2 * channels // 8 // 16) * 16
    atm = atm_state.reshape(channels_a * rows_a, lanes)
    ocean = ocean_state.reshape(channels_o * rows_o, lanes)
    mask = ocean_mask.reshape(1, rows_o)
    routes = tile_pairs(tile_count)
    even_pairs, odd_pairs = comp_pairs(lax.axis_size("comp"))

    hbm = lambda x: pltpu.with_memory_space_constraint(x, pltpu.HBM)
    surface, wet = call(
        functools.partial(pack_surface, rows_a, rows_o),
        0.8,
        4 << 20,
        in_specs=[HBM] * 3,
        out_specs=[VMEM, SMEM],
        out_shape=[
            pltpu.VMEM((block, SURF, lanes), BF16),
            pltpu.SMEM((1, rows_o), jnp.int32),
        ],
        scratch_shapes=[
            pltpu.VMEM((SURF * rows_a, lanes), F32),
            pltpu.VMEM((SURF * rows_o, lanes), F32),
            pltpu.SemaphoreType.DMA((3,)),
        ],
        name="pack_surface",
    )(hbm(atm), hbm(ocean), hbm(mask))
    received = exchange([surface] * len(routes), routes)

    halo = pltpu.VMEM((2, channels, lanes), BF16)
    atm, ocean, even_rows, odd_rows, rate, table, live = call(
        functools.partial(prepare, rows_a, rows_o),
        1.5,
        8 << 20,
        in_specs=[HBM, HBM, SMEM] + [HBM] * 4,
        out_specs=[VMEM] * 5 + [SMEM] * 2,
        out_shape=[
            pltpu.VMEM(atm.shape, F32),
            pltpu.VMEM(ocean.shape, F32),
            halo,
            halo,
            pltpu.VMEM((channels, lanes), F32),
            pltpu.SMEM((2, pair_src.shape[1]), jnp.int32),
            pltpu.SMEM((1, pair_src.shape[1]), jnp.int32),
        ],
        scratch_shapes=[
            pltpu.VMEM((1, channels_a), F32),
            pltpu.VMEM((1, channels_o), F32),
            pltpu.SemaphoreType.DMA((6,)),
        ],
        name="prepare",
    )(
        hbm(atm),
        hbm(ocean),
        pair_count,
        hbm(pair_src),
        hbm(pair_tgt),
        hbm(atm_rate.reshape(1, channels_a)),
        hbm(ocean_rate.reshape(1, channels_o)),
    )
    even_in = lax.ppermute(even_rows, "comp", even_pairs)
    odd_in = lax.ppermute(odd_rows, "comp", odd_pairs)

    sends = [jax.ShapeDtypeStruct((message + extra, lanes), BF16)] * 2
    sends += [jax.ShapeDtypeStruct((message, lanes), BF16)] * (tile_count - 3)
    own_part, *parts = call(
        functools.partial(remap, tile_count, rows_a, rows_o),
        2.0,
        12 << 20,
        in_specs=[SMEM, SMEM] + [VMEM] * (1 + tile_count),
        out_specs=[VMEM] * tile_count,
        out_shape=[jax.ShapeDtypeStruct((block, SURF, lanes), F32)] + sends,
        scratch_shapes=[
            pltpu.VMEM((tile_count * block, SURF, lanes), BF16),
            pltpu.VMEM((tile_count * block, SURF, lanes), F32),
        ],
        name="remap",
    )(table, live, remap_weight[0], surface, *received)
    parts[:2] = call(
        functools.partial(pack_columns, rows_a, rows_o),
        1.2,
        8 << 20,
        in_specs=[VMEM] * 7,
        out_specs=[VMEM, VMEM],
        out_shape=sends[:2],
        input_output_aliases={5: 0, 6: 1},
        scratch_shapes=[
            pltpu.VMEM((channels_a * rows_a + channels_o * rows_o, lanes), F32),
            pltpu.VMEM((2, extra, lanes), F32),
        ],
        name="pack_columns",
    )(atm, ocean, rate, even_in, odd_in, *parts[:2])
    returned = exchange(parts, routes)

    atm_base, ocean_base = call(
        functools.partial(stencil, rows_a, rows_o),
        2.5,
        8 << 20,
        in_specs=[VMEM] * 5,
        out_specs=[VMEM, VMEM],
        out_shape=[
            jax.ShapeDtypeStruct(atm.shape, F32),
            jax.ShapeDtypeStruct(ocean.shape, F32),
        ],
        name="stencil",
    )(atm, ocean, rate, even_in, odd_in)

    atm_next, ocean_next = call(
        functools.partial(final, tile_count, rows_a, rows_o),
        2.0,
        12 << 20,
        in_specs=[SMEM] + [VMEM] * (2 + tile_count),
        out_specs=[HBM, HBM],
        out_shape=[
            jax.ShapeDtypeStruct(atm.shape, F32),
            jax.ShapeDtypeStruct(ocean.shape, F32),
        ],
        scratch_shapes=[
            pltpu.VMEM((SURF * block, lanes), F32),
            pltpu.VMEM(atm.shape, F32),
            pltpu.VMEM(ocean.shape, F32),
            pltpu.SemaphoreType.DMA((channels // 8,)),
        ],
        name="final",
    )(wet, atm_base, ocean_base, own_part, *returned)
    return (
        atm_next.reshape(channels_a, rows_a, lanes),
        ocean_next.reshape(channels_o, rows_o, lanes),
    )


def solution(mesh):
    return jax.shard_map(
        interval,
        mesh=mesh,
        in_specs=(
            P(None, "comp", "tile"),
            P(None, "comp", "tile"),
            P(),
            P(),
            P("comp", "tile"),
            P("comp", "tile", None, None),
            P("comp", "tile"),
            P("comp", "tile"),
            P("comp", "tile"),
        ),
        out_specs=(P(None, "comp", "tile"), P(None, "comp", "tile")),
        check_vma=False,
    )
```

```python
import functools

import jax
import jax.numpy as jnp
from jax import lax
from jax.experimental import pallas as pl
from jax.experimental.pallas import tpu as pltpu
from jax.sharding import PartitionSpec as P


SURF = 8
F32 = jnp.float32
BF16 = jnp.bfloat16
VMEM = pl.BlockSpec(memory_space=pltpu.VMEM)
SMEM = pl.BlockSpec(memory_space=pltpu.SMEM)
HBM = pl.BlockSpec(memory_space=pltpu.HBM)
ANY = pl.BlockSpec(memory_space=pl.ANY)


def beside_even(index):
    return index + 1 - 2 * (index % 2)


def beside_odd(index, count):
    return (index - 1 + 2 * (index % 2) + count) % count


def tile_pairs(count):
    routes = [
        [(i, beside_even(i)) for i in range(count)],
        [(i, beside_odd(i, count)) for i in range(count)],
    ]
    routes += [[(i, (i + s) % count) for i in range(count)] for s in range(2, count - 1)]
    return routes


def peers(me, count):
    a = beside_even(me)
    b = beside_odd(me, count)
    far = range(2, count - 1)
    sources = [a, b] + [lax.rem(me - s + count, count) for s in far]
    targets = [a, b] + [lax.rem(me + s, count) for s in far]
    return sources, targets


def comp_pairs(count):
    even = [(i, beside_even(i)) for i in range(count)]
    odd = [(i, i + 1) for i in range(1, count - 1, 2)] + [(i + 1, i) for i in range(1, count - 1, 2)]
    return even, odd


def pack_surface(rows_a, rows_o, *refs):
    atm_in, ocean_in, mask_in, src_in, tgt_in, rate_a_in, rate_o_in = refs[:7]
    surface, rate_a, rate_o, table, mask, atm, ocean, done = refs[7:]
    copies = [
        (mask_in, mask),
        (atm_in.at[0 : SURF * rows_a], atm),
        (ocean_in.at[0 : SURF * rows_o], ocean),
        (src_in, table.at[0:1]),
        (tgt_in, table.at[1:2]),
        (rate_a_in, rate_a),
        (rate_o_in, rate_o),
    ]
    copies = [pltpu.make_async_copy(a, b, done.at[i]) for i, (a, b) in enumerate(copies)]
    for copy in copies:
        copy.start()
    copies[1].wait()
    for y in range(rows_a):
        surface[y] = atm[pl.ds(y, SURF, stride=rows_a), :].astype(BF16)
    copies[0].wait()
    copies[2].wait()
    for y in range(rows_o):
        tile = ocean[pl.ds(y, SURF, stride=rows_o), :]
        surface[rows_a + y] = (tile * mask[0, y].astype(F32)).astype(BF16)
    for copy in copies[3:]:
        copy.wait()


def prepare(rows_a, rows_o, *refs):
    atm, ocean, number, _, rate_a, rate_o = refs[:6]
    even_out, odd_out, rate, live = refs[6:]
    live[0, 0] = number[0, 0]
    parity = lax.rem(lax.axis_index("comp"), 2)
    at = 0
    for ref, rows in ((atm, rows_a), (ocean, rows_o)):
        channels = ref.shape[0] // rows
        for c in range(0, channels, 8):
            for r in range(2):
                low = ref[pl.ds(c * rows + r, 8, stride=rows), :]
                high = ref[pl.ds(c * rows + rows - 2 + r, 8, stride=rows), :]
                even_out[r, at + c : at + c + 8, :] = jnp.where(parity == 0, high, low).astype(BF16)
                odd_out[r, at + c : at + c + 8, :] = jnp.where(parity == 0, low, high).astype(BF16)
        at += channels
    lanes = atm.shape[1]
    split = rate_a.shape[1]
    rate[0:split, :] = jnp.broadcast_to(rate_a[...], (lanes, split)).T
    rate[split:, :] = jnp.broadcast_to(rate_o[...], (lanes, rate_o.shape[1])).T


def halo_rows(parity, even_in, odd_in, at):
    e = [even_in[r, at : at + 8, :].astype(F32) for r in range(2)]
    o = [odd_in[r, at : at + 8, :].astype(F32) for r in range(2)]
    north = [jnp.where(parity == 0, o[r], e[r]) for r in range(2)]
    south = [jnp.where(parity == 0, e[r], o[r]) for r in range(2)]
    return north, south


def pack_columns(rows_a, rows_o, atm, ocean, rate, even_in, odd_in, part_a, part_b, out_a, out_b, spread, stage):
    del part_a, part_b
    parity = lax.rem(lax.axis_index("comp"), 2)
    tile_parity = lax.rem(lax.axis_index("tile"), 2)
    lanes = atm.shape[1]
    row = lax.broadcasted_iota(jnp.int32, (8, lanes), 0)
    lane = lax.broadcasted_iota(jnp.int32, (8, lanes), 1)
    east = lax.div(row, 2) == tile_parity
    second = lax.rem(row, 2)
    spot = jnp.where(east, lanes - 1 - second, second)
    pick = jnp.where((row < 4) & (lane == spot), 1.0, 0.0).astype(BF16)
    outer = (lane == 0) | (lane == lanes - 1)
    turn = (lane == 1) | (lane == lanes - 1)
    dims = (((1,), (1,)), ((), ()))
    stage[...] = jnp.zeros_like(stage)
    at = 0
    for ref, rows in ((atm, rows_a), (ocean, rows_o)):
        channels = ref.shape[0] // rows
        for c in range(0, channels, 8):
            rho = rate[at + c : at + c + 8, :]
            own = 2.0 * rho * (1.0 - 4.0 * rho)
            square = rho * rho
            north, south = halo_rows(parity, even_in, odd_in, at + c)
            q = [north[1]]
            q += [ref[pl.ds(c * rows + r, 8, stride=rows), :] for r in range(rows)]
            q += [south[0]]
            for r in range(rows):
                far = square * q[r + 1]
                near = own * q[r + 1] + 2.0 * square * (q[r] + q[r + 2])
                moved = jnp.where(turn, pltpu.roll(far, 1, 1), pltpu.roll(far, lanes - 1, 1))
                value = moved + jnp.where(outer, near, 0.0)
                spread[pl.ds((at + c) * rows + r, 8, stride=rows), :] = value
        at += channels
    for j in range(at // 8):
        part = spread[j * 8 * rows_a : (j + 1) * 8 * rows_a, :].astype(BF16)
        found = lax.dot_general(pick, part, dims, preferred_element_type=F32)
        stage[0, 2 * j : 2 * j + 2, :] = found[0:2, :]
        stage[1, 2 * j : 2 * j + 2, :] = found[2:4, :]
    behind = out_a.shape[0] - stage.shape[1]
    out_a[behind:, :] = stage[0].astype(BF16)
    out_b[behind:, :] = stage[1].astype(BF16)


def remap(tile_count, rows_a, rows_o, *refs):
    table, number, weights, own = refs[:4]
    got = refs[4 : 3 + tile_count]
    own_out = refs[3 + tile_count]
    outs = refs[4 + tile_count : 3 + 2 * tile_count]
    band, total = refs[3 + 2 * tile_count :]
    block = rows_a + rows_o
    me = lax.axis_index("tile")
    sources, targets = peers(me, tile_count)
    band[pl.ds(me * block, block)] = own[...]
    for e, ref in zip(sources, got):
        band[pl.ds(e * block, block)] = ref[...]
    total[...] = jnp.zeros_like(total)
    pairs = weights.shape[0]
    live_count = number[0, 0]
    trans = (((1,), (1,)), ((), ()))
    plain = (((1,), (0,)), ((), ()))
    group = 8
    for start in range(0, pairs, group):
        made = []
        for k in range(start, min(start + group, pairs)):
            a = table[0, k]
            o = table[1, k]
            at_a = lax.div(a, rows_a) * block + lax.rem(a, rows_a)
            at_o = lax.div(o, rows_o) * block + rows_a + lax.rem(o, rows_o)
            live = k < live_count
            w = weights[k]
            ta = band[at_a]
            to = band[at_o]
            ta = jnp.where(live, ta, jnp.zeros_like(ta))
            to = jnp.where(live, to, jnp.zeros_like(to))
            ahead = lax.dot_general(ta, w, plain, preferred_element_type=F32)
            back = lax.dot_general(to, w, trans, preferred_element_type=F32)
            made.append((at_a, at_o, ahead, back))
        for at_a, at_o, ahead, back in made:
            total[at_o] += ahead
            total[at_a] += back
    own_out[...] = total[pl.ds(me * block, block)]
    lanes = weights.shape[2]
    for e, ref in zip(targets, outs):
        part = total[pl.ds(e * block, block)].astype(BF16)
        ref[0 : block * SURF, :] = part.reshape(block * SURF, lanes)


def stencil(rows_a, rows_o, atm, ocean, rate, even_in, odd_in, atm_out, ocean_out):
    comp = lax.axis_index("comp")
    parity = lax.rem(comp, 2)
    lanes = atm.shape[1]
    lane = lax.broadcasted_iota(jnp.int32, (8, lanes), 1)
    at_west = lane == 0
    at_east = lane == lanes - 1
    keep_north = jnp.where(comp == 0, 0.0, 1.0).astype(F32)
    keep_south = jnp.where(comp == lax.axis_size("comp") - 1, 0.0, 1.0).astype(F32)
    at = 0
    for ref, rows, out in ((atm, rows_a, atm_out), (ocean, rows_o, ocean_out)):
        channels = ref.shape[0] // rows
        for c in range(0, channels, 8):
            rho = rate[at + c : at + c + 8, :]
            own = 1.0 - 4.0 * rho
            north, south = halo_rows(parity, even_in, odd_in, at + c)
            q = north + [ref[pl.ds(c * rows + r, 8, stride=rows), :] for r in range(rows)] + south
            p = []
            for i in range(1, rows + 3):
                west = jnp.where(at_west, 0.0, pltpu.roll(q[i], 1, 1))
                east = jnp.where(at_east, 0.0, pltpu.roll(q[i], lanes - 1, 1))
                p.append(own * q[i] + rho * ((q[i - 1] + q[i + 1]) + (west + east)))
            p[0] = p[0] * keep_north
            p[rows + 1] = p[rows + 1] * keep_south
            for r in range(rows):
                ghost = rho * q[r + 2]
                west = jnp.where(at_west, ghost, pltpu.roll(p[r + 1], 1, 1))
                east = jnp.where(at_east, ghost, pltpu.roll(p[r + 1], lanes - 1, 1))
                out[pl.ds(c * rows + r, 8, stride=rows), :] = own * p[r + 1] + rho * (
                    (p[r] + p[r + 2]) + (west + east)
                )
        at += channels


def final(tile_count, rows_a, rows_o, *refs):
    mask, atm, ocean, own = refs[:4]
    got = refs[4 : 3 + tile_count]
    atm_out, ocean_out, force, value_a, value_o, done = refs[3 + tile_count :]
    lanes = atm.shape[1]
    block = rows_a + rows_o
    message = block * SURF
    tile_parity = lax.rem(lax.axis_index("tile"), 2)
    row = lax.broadcasted_iota(jnp.int32, (8, lanes), 0)
    lane = lax.broadcasted_iota(jnp.int32, (8, lanes), 1)
    east = lax.div(row, 2) == tile_parity
    second = lax.rem(row, 2)
    spot = jnp.where(east, lanes - 1 - second, second)
    place = jnp.where((row < 4) & (lane == spot), 1.0, 0.0).astype(BF16)
    for y in range(block):
        total = own[y]
        for ref in got:
            total = total + ref[SURF * y : SURF * y + SURF, :].astype(F32)
        if y >= rows_a:
            total = total * mask[0, y - rows_a].astype(F32)
        start = y if y < rows_a else SURF * rows_a + y - rows_a
        force[pl.ds(start, SURF, stride=rows_a if y < rows_a else rows_o), :] = total
    dims = (((0,), (0,)), ((), ()))
    group = 32
    at = 0
    copies = []
    for ref, keep, out, rows, add in (
        (atm, value_a, atm_out, rows_a, 0),
        (ocean, value_o, ocean_out, rows_o, SURF * rows_a),
    ):
        channels = ref.shape[0] // rows
        for c in range(0, channels, 8):
            j = message + 2 * ((at + c) // 8)
            sides = jnp.concatenate(
                [
                    got[0][j : j + 2, :].astype(F32),
                    got[1][j : j + 2, :].astype(F32),
                    jnp.zeros((4, lanes), F32),
                ],
                axis=0,
            ).astype(BF16)
            value = ref[c * rows : (c + 8) * rows, :] + lax.dot_general(
                sides, place, dims, preferred_element_type=F32
            )
            if c == 0:
                value = value + force[add : add + SURF * rows, :]
            keep[c * rows : (c + 8) * rows, :] = value
            if (c + 8) % group == 0 or c + 8 == channels:
                begin = c // group * group * rows
                end = (c + 8) * rows
                copies.append(
                    pltpu.make_async_copy(
                        keep.at[begin:end], out.at[begin:end], done.at[len(copies)]
                    )
                )
                copies[-1].start()
        at += channels
    for copy in copies:
        copy.wait()


def call(body, micros, limit, **rest):
    return pl.pallas_call(
        body,
        compiler_params=pltpu.CompilerParams(vmem_limit_bytes=limit),
        cost_estimate=pl.CostEstimate(
            flops=0, transcendentals=0, bytes_accessed=int(micros * 3.0e6)
        ),
        **rest,
    )


def exchange(blocks, routes):
    out = []
    for block, route in zip(blocks, routes):
        out.append(lax.ppermute(block, "tile", route))
    return out


def interval(
    atm_state,
    ocean_state,
    atm_rate,
    ocean_rate,
    ocean_mask,
    remap_weight,
    pair_src,
    pair_tgt,
    pair_count,
):
    channels_a, rows_a, lanes = atm_state.shape
    channels_o, rows_o, _ = ocean_state.shape
    channels = channels_a + channels_o
    tile_count = lax.axis_size("tile")
    block = rows_a + rows_o
    message = block * SURF
    extra = -(-2 * channels // 8 // 16) * 16
    atm = atm_state.reshape(channels_a * rows_a, lanes)
    ocean = ocean_state.reshape(channels_o * rows_o, lanes)
    mask = ocean_mask.reshape(1, rows_o)
    routes = tile_pairs(tile_count)
    even_pairs, odd_pairs = comp_pairs(lax.axis_size("comp"))

    hbm = lambda x: pltpu.with_memory_space_constraint(x, pltpu.HBM)
    surface, rate_a, rate_o, table, wet = call(
        functools.partial(pack_surface, rows_a, rows_o),
        0.8,
        4 << 20,
        in_specs=[HBM] * 7,
        out_specs=[VMEM] * 3 + [SMEM] * 2,
        out_shape=[
            pltpu.VMEM((block, SURF, lanes), BF16),
            pltpu.VMEM((1, channels_a), F32),
            pltpu.VMEM((1, channels_o), F32),
            pltpu.SMEM((2, pair_src.shape[1]), jnp.int32),
            pltpu.SMEM((1, rows_o), jnp.int32),
        ],
        scratch_shapes=[
            pltpu.VMEM((SURF * rows_a, lanes), F32),
            pltpu.VMEM((SURF * rows_o, lanes), F32),
            pltpu.SemaphoreType.DMA((7,)),
        ],
        name="pack_surface",
    )(
        hbm(atm),
        hbm(ocean),
        hbm(mask),
        hbm(pair_src),
        hbm(pair_tgt),
        hbm(atm_rate.reshape(1, channels_a)),
        hbm(ocean_rate.reshape(1, channels_o)),
    )
    received = exchange([surface] * len(routes), routes)

    halo = pltpu.VMEM((2, channels, lanes), BF16)
    even_rows, odd_rows, rate, live = call(
        functools.partial(prepare, rows_a, rows_o),
        0.5,
        4 << 20,
        in_specs=[VMEM, VMEM, SMEM, HBM, VMEM, VMEM],
        out_specs=[VMEM] * 3 + [SMEM],
        out_shape=[
            halo,
            halo,
            pltpu.VMEM((channels, lanes), F32),
            pltpu.SMEM((1, pair_src.shape[1]), jnp.int32),
        ],
        name="prepare",
    )(atm, ocean, pair_count, hbm(remap_weight[0]), rate_a, rate_o)
    even_in = lax.ppermute(even_rows, "comp", even_pairs)
    odd_in = lax.ppermute(odd_rows, "comp", odd_pairs)

    sends = [jax.ShapeDtypeStruct((message + extra, lanes), BF16)] * 2
    sends += [jax.ShapeDtypeStruct((message, lanes), BF16)] * (tile_count - 3)
    own_part, *parts = call(
        functools.partial(remap, tile_count, rows_a, rows_o),
        2.0,
        12 << 20,
        in_specs=[SMEM, SMEM] + [VMEM] * (1 + tile_count),
        out_specs=[VMEM] * tile_count,
        out_shape=[jax.ShapeDtypeStruct((block, SURF, lanes), F32)] + sends,
        scratch_shapes=[
            pltpu.VMEM((tile_count * block, SURF, lanes), BF16),
            pltpu.VMEM((tile_count * block, SURF, lanes), F32),
        ],
        name="remap",
    )(table, live, remap_weight[0], surface, *received)
    parts[:2] = call(
        functools.partial(pack_columns, rows_a, rows_o),
        1.2,
        8 << 20,
        in_specs=[VMEM] * 7,
        out_specs=[VMEM, VMEM],
        out_shape=sends[:2],
        input_output_aliases={5: 0, 6: 1},
        scratch_shapes=[
            pltpu.VMEM((channels_a * rows_a + channels_o * rows_o, lanes), F32),
            pltpu.VMEM((2, extra, lanes), F32),
        ],
        name="pack_columns",
    )(atm, ocean, rate, even_in, odd_in, *parts[:2])
    returned = exchange(parts, routes)

    atm_base, ocean_base = call(
        functools.partial(stencil, rows_a, rows_o),
        2.5,
        8 << 20,
        in_specs=[VMEM] * 5,
        out_specs=[VMEM, VMEM],
        out_shape=[
            jax.ShapeDtypeStruct(atm.shape, F32),
            jax.ShapeDtypeStruct(ocean.shape, F32),
        ],
        name="stencil",
    )(atm, ocean, rate, even_in, odd_in)

    atm_next, ocean_next = call(
        functools.partial(final, tile_count, rows_a, rows_o),
        2.0,
        12 << 20,
        in_specs=[SMEM] + [VMEM] * (2 + tile_count),
        out_specs=[HBM, HBM],
        out_shape=[
            jax.ShapeDtypeStruct(atm.shape, F32),
            jax.ShapeDtypeStruct(ocean.shape, F32),
        ],
        scratch_shapes=[
            pltpu.VMEM((SURF * block, lanes), F32),
            pltpu.VMEM(atm.shape, F32),
            pltpu.VMEM(ocean.shape, F32),
            pltpu.SemaphoreType.DMA((channels // 8,)),
        ],
        name="final",
    )(wet, atm_base, ocean_base, own_part, *returned)
    return (
        atm_next.reshape(channels_a, rows_a, lanes),
        ocean_next.reshape(channels_o, rows_o, lanes),
    )


def solution(mesh):
    return jax.shard_map(
        interval,
        mesh=mesh,
        in_specs=(
            P(None, "comp", "tile"),
            P(None, "comp", "tile"),
            P(),
            P(),
            P("comp", "tile"),
            P("comp", "tile", None, None),
            P("comp", "tile"),
            P("comp", "tile"),
            P("comp", "tile"),
        ),
        out_specs=(P(None, "comp", "tile"), P(None, "comp", "tile")),
        check_vma=False,
    )
```

```python
import functools

import jax
import jax.numpy as jnp
from jax import lax
from jax.experimental import pallas as pl
from jax.experimental.pallas import tpu as pltpu
from jax.sharding import PartitionSpec as P


SURF = 8
F32 = jnp.float32
BF16 = jnp.bfloat16
VMEM = pl.BlockSpec(memory_space=pltpu.VMEM)
SMEM = pl.BlockSpec(memory_space=pltpu.SMEM)
HBM = pl.BlockSpec(memory_space=pltpu.HBM)
ANY = pl.BlockSpec(memory_space=pl.ANY)


def beside_even(index):
    return index + 1 - 2 * (index % 2)


def beside_odd(index, count):
    return (index - 1 + 2 * (index % 2) + count) % count


def tile_pairs(count):
    routes = [
        [(i, beside_even(i)) for i in range(count)],
        [(i, beside_odd(i, count)) for i in range(count)],
    ]
    routes += [[(i, (i + s) % count) for i in range(count)] for s in range(2, count - 1)]
    return routes


def peers(me, count):
    a = beside_even(me)
    b = beside_odd(me, count)
    far = range(2, count - 1)
    sources = [a, b] + [lax.rem(me - s + count, count) for s in far]
    targets = [a, b] + [lax.rem(me + s, count) for s in far]
    return sources, targets


def comp_pairs(count):
    even = [(i, beside_even(i)) for i in range(count)]
    odd = [(i, beside_odd(i, count)) for i in range(count)]
    return even, odd


def pack_surface(rows_a, rows_o, *refs):
    atm_in, ocean_in, mask_in, src_in, tgt_in, rate_a_in, rate_o_in = refs[:7]
    surface, rate_a, rate_o, table, mask, atm, ocean, done = refs[7:]
    copies = [
        (mask_in, mask),
        (atm_in.at[0 : SURF * rows_a], atm),
        (ocean_in.at[0 : SURF * rows_o], ocean),
        (src_in, table.at[0:1]),
        (tgt_in, table.at[1:2]),
        (rate_a_in, rate_a),
        (rate_o_in, rate_o),
    ]
    copies = [pltpu.make_async_copy(a, b, done.at[i]) for i, (a, b) in enumerate(copies)]
    for copy in copies:
        copy.start()
    copies[1].wait()
    for y in range(rows_a):
        surface[y] = atm[pl.ds(y, SURF, stride=rows_a), :].astype(BF16)
    copies[0].wait()
    copies[2].wait()
    for y in range(rows_o):
        tile = ocean[pl.ds(y, SURF, stride=rows_o), :]
        surface[rows_a + y] = (tile * mask[0, y].astype(F32)).astype(BF16)
    for copy in copies[3:]:
        copy.wait()


def prepare(rows_a, rows_o, *refs):
    atm, ocean, number, _, rate_a, rate_o = refs[:6]
    even_out, odd_out, rate, live = refs[6:]
    live[0, 0] = number[0, 0]
    parity = lax.rem(lax.axis_index("comp"), 2)
    at = 0
    for ref, rows in ((atm, rows_a), (ocean, rows_o)):
        channels = ref.shape[0] // rows
        for c in range(0, channels, 8):
            for r in range(2):
                low = ref[pl.ds(c * rows + r, 8, stride=rows), :]
                high = ref[pl.ds(c * rows + rows - 2 + r, 8, stride=rows), :]
                even_out[r, at + c : at + c + 8, :] = jnp.where(parity == 0, high, low).astype(BF16)
                odd_out[r, at + c : at + c + 8, :] = jnp.where(parity == 0, low, high).astype(BF16)
        at += channels
    lanes = atm.shape[1]
    split = rate_a.shape[1]
    rate[0:split, :] = jnp.broadcast_to(rate_a[...], (lanes, split)).T
    rate[split:, :] = jnp.broadcast_to(rate_o[...], (lanes, rate_o.shape[1])).T


def halo_rows(comp, even_in, odd_in, at):
    parity = lax.rem(comp, 2)
    outside = (comp == 0) | (comp == lax.axis_size("comp") - 1)
    e = [even_in[r, at : at + 8, :].astype(F32) for r in range(2)]
    o = [odd_in[r, at : at + 8, :].astype(F32) for r in range(2)]
    o = [jnp.where(outside, jnp.zeros_like(x), x) for x in o]
    north = [jnp.where(parity == 0, o[r], e[r]) for r in range(2)]
    south = [jnp.where(parity == 0, e[r], o[r]) for r in range(2)]
    return north, south


def pack_columns(rows_a, rows_o, atm, ocean, rate, even_in, odd_in, part_a, part_b, out_a, out_b, spread, stage):
    del part_a, part_b
    comp = lax.axis_index("comp")
    tile_parity = lax.rem(lax.axis_index("tile"), 2)
    lanes = atm.shape[1]
    row = lax.broadcasted_iota(jnp.int32, (8, lanes), 0)
    lane = lax.broadcasted_iota(jnp.int32, (8, lanes), 1)
    east = lax.div(row, 2) == tile_parity
    second = lax.rem(row, 2)
    spot = jnp.where(east, lanes - 1 - second, second)
    pick = jnp.where((row < 4) & (lane == spot), 1.0, 0.0).astype(BF16)
    outer = (lane == 0) | (lane == lanes - 1)
    turn = (lane == 1) | (lane == lanes - 1)
    dims = (((1,), (1,)), ((), ()))
    stage[...] = jnp.zeros_like(stage)
    at = 0
    for ref, rows in ((atm, rows_a), (ocean, rows_o)):
        channels = ref.shape[0] // rows
        for c in range(0, channels, 8):
            rho = rate[at + c : at + c + 8, :]
            own = 2.0 * rho * (1.0 - 4.0 * rho)
            square = rho * rho
            north, south = halo_rows(comp, even_in, odd_in, at + c)
            q = [north[1]]
            q += [ref[pl.ds(c * rows + r, 8, stride=rows), :] for r in range(rows)]
            q += [south[0]]
            for r in range(rows):
                far = square * q[r + 1]
                near = own * q[r + 1] + 2.0 * square * (q[r] + q[r + 2])
                moved = jnp.where(turn, pltpu.roll(far, 1, 1), pltpu.roll(far, lanes - 1, 1))
                value = moved + jnp.where(outer, near, 0.0)
                spread[pl.ds((at + c) * rows + r, 8, stride=rows), :] = value
        at += channels
    for j in range(at // 8):
        part = spread[j * 8 * rows_a : (j + 1) * 8 * rows_a, :].astype(BF16)
        found = lax.dot_general(pick, part, dims, preferred_element_type=F32)
        stage[0, 2 * j : 2 * j + 2, :] = found[0:2, :]
        stage[1, 2 * j : 2 * j + 2, :] = found[2:4, :]
    behind = out_a.shape[0] - stage.shape[1]
    out_a[behind:, :] = stage[0].astype(BF16)
    out_b[behind:, :] = stage[1].astype(BF16)


def remap(tile_count, rows_a, rows_o, *refs):
    table, number, weights, own = refs[:4]
    got = refs[4 : 3 + tile_count]
    own_out = refs[3 + tile_count]
    outs = refs[4 + tile_count : 3 + 2 * tile_count]
    band, total = refs[3 + 2 * tile_count :]
    block = rows_a + rows_o
    me = lax.axis_index("tile")
    sources, targets = peers(me, tile_count)
    band[pl.ds(me * block, block)] = own[...]
    for e, ref in zip(sources, got):
        band[pl.ds(e * block, block)] = ref[...]
    total[...] = jnp.zeros_like(total)
    pairs = weights.shape[0]
    live_count = number[0, 0]
    trans = (((1,), (1,)), ((), ()))
    plain = (((1,), (0,)), ((), ()))
    group = 8
    for start in range(0, pairs, group):
        made = []
        for k in range(start, min(start + group, pairs)):
            a = table[0, k]
            o = table[1, k]
            at_a = lax.div(a, rows_a) * block + lax.rem(a, rows_a)
            at_o = lax.div(o, rows_o) * block + rows_a + lax.rem(o, rows_o)
            live = k < live_count
            w = weights[k]
            ta = band[at_a]
            to = band[at_o]
            ta = jnp.where(live, ta, jnp.zeros_like(ta))
            to = jnp.where(live, to, jnp.zeros_like(to))
            ahead = lax.dot_general(ta, w, plain, preferred_element_type=F32)
            back = lax.dot_general(to, w, trans, preferred_element_type=F32)
            made.append((at_a, at_o, ahead, back))
        for at_a, at_o, ahead, back in made:
            total[at_o] += ahead
            total[at_a] += back
    own_out[...] = total[pl.ds(me * block, block)]
    lanes = weights.shape[2]
    for e, ref in zip(targets, outs):
        part = total[pl.ds(e * block, block)].astype(BF16)
        ref[0 : block * SURF, :] = part.reshape(block * SURF, lanes)


def stencil(rows_a, rows_o, atm, ocean, rate, even_in, odd_in, atm_out, ocean_out):
    comp = lax.axis_index("comp")
    lanes = atm.shape[1]
    lane = lax.broadcasted_iota(jnp.int32, (8, lanes), 1)
    at_west = lane == 0
    at_east = lane == lanes - 1
    keep_north = jnp.where(comp == 0, 0.0, 1.0).astype(F32)
    keep_south = jnp.where(comp == lax.axis_size("comp") - 1, 0.0, 1.0).astype(F32)
    at = 0
    for ref, rows, out in ((atm, rows_a, atm_out), (ocean, rows_o, ocean_out)):
        channels = ref.shape[0] // rows
        for c in range(0, channels, 8):
            rho = rate[at + c : at + c + 8, :]
            own = 1.0 - 4.0 * rho
            north, south = halo_rows(comp, even_in, odd_in, at + c)
            q = north + [ref[pl.ds(c * rows + r, 8, stride=rows), :] for r in range(rows)] + south
            p = []
            for i in range(1, rows + 3):
                west = jnp.where(at_west, 0.0, pltpu.roll(q[i], 1, 1))
                east = jnp.where(at_east, 0.0, pltpu.roll(q[i], lanes - 1, 1))
                p.append(own * q[i] + rho * ((q[i - 1] + q[i + 1]) + (west + east)))
            p[0] = p[0] * keep_north
            p[rows + 1] = p[rows + 1] * keep_south
            for r in range(rows):
                ghost = rho * q[r + 2]
                west = jnp.where(at_west, ghost, pltpu.roll(p[r + 1], 1, 1))
                east = jnp.where(at_east, ghost, pltpu.roll(p[r + 1], lanes - 1, 1))
                out[pl.ds(c * rows + r, 8, stride=rows), :] = own * p[r + 1] + rho * (
                    (p[r] + p[r + 2]) + (west + east)
                )
        at += channels


def final(tile_count, rows_a, rows_o, *refs):
    mask, atm, ocean, own = refs[:4]
    got = refs[4 : 3 + tile_count]
    atm_out, ocean_out, force, value_a, value_o, done = refs[3 + tile_count :]
    lanes = atm.shape[1]
    block = rows_a + rows_o
    message = block * SURF
    tile_parity = lax.rem(lax.axis_index("tile"), 2)
    row = lax.broadcasted_iota(jnp.int32, (8, lanes), 0)
    lane = lax.broadcasted_iota(jnp.int32, (8, lanes), 1)
    east = lax.div(row, 2) == tile_parity
    second = lax.rem(row, 2)
    spot = jnp.where(east, lanes - 1 - second, second)
    place = jnp.where((row < 4) & (lane == spot), 1.0, 0.0).astype(BF16)
    for y in range(block):
        total = own[y]
        for ref in got:
            total = total + ref[SURF * y : SURF * y + SURF, :].astype(F32)
        if y >= rows_a:
            total = total * mask[0, y - rows_a].astype(F32)
        start = y if y < rows_a else SURF * rows_a + y - rows_a
        force[pl.ds(start, SURF, stride=rows_a if y < rows_a else rows_o), :] = total
    dims = (((0,), (0,)), ((), ()))
    group = 32
    at = 0
    copies = []
    for ref, keep, out, rows, add in (
        (atm, value_a, atm_out, rows_a, 0),
        (ocean, value_o, ocean_out, rows_o, SURF * rows_a),
    ):
        channels = ref.shape[0] // rows
        for c in range(0, channels, 8):
            j = message + 2 * ((at + c) // 8)
            sides = jnp.concatenate(
                [
                    got[0][j : j + 2, :].astype(F32),
                    got[1][j : j + 2, :].astype(F32),
                    jnp.zeros((4, lanes), F32),
                ],
                axis=0,
            ).astype(BF16)
            value = ref[c * rows : (c + 8) * rows, :] + lax.dot_general(
                sides, place, dims, preferred_element_type=F32
            )
            if c == 0:
                value = value + force[add : add + SURF * rows, :]
            keep[c * rows : (c + 8) * rows, :] = value
            if (c + 8) % group == 0 or c + 8 == channels:
                begin = c // group * group * rows
                end = (c + 8) * rows
                copies.append(
                    pltpu.make_async_copy(
                        keep.at[begin:end], out.at[begin:end], done.at[len(copies)]
                    )
                )
                copies[-1].start()
        at += channels
    for copy in copies:
        copy.wait()


def call(body, micros, limit, **rest):
    return pl.pallas_call(
        body,
        compiler_params=pltpu.CompilerParams(vmem_limit_bytes=limit),
        cost_estimate=pl.CostEstimate(
            flops=0, transcendentals=0, bytes_accessed=int(micros * 3.0e6)
        ),
        **rest,
    )


def exchange(blocks, routes):
    out = []
    for block, route in zip(blocks, routes):
        out.append(lax.ppermute(block, "tile", route))
    return out


def interval(
    atm_state,
    ocean_state,
    atm_rate,
    ocean_rate,
    ocean_mask,
    remap_weight,
    pair_src,
    pair_tgt,
    pair_count,
):
    channels_a, rows_a, lanes = atm_state.shape
    channels_o, rows_o, _ = ocean_state.shape
    channels = channels_a + channels_o
    tile_count = lax.axis_size("tile")
    block = rows_a + rows_o
    message = block * SURF
    extra = -(-2 * channels // 8 // 16) * 16
    atm = atm_state.reshape(channels_a * rows_a, lanes)
    ocean = ocean_state.reshape(channels_o * rows_o, lanes)
    mask = ocean_mask.reshape(1, rows_o)
    routes = tile_pairs(tile_count)
    even_pairs, odd_pairs = comp_pairs(lax.axis_size("comp"))

    hbm = lambda x: pltpu.with_memory_space_constraint(x, pltpu.HBM)
    surface, rate_a, rate_o, table, wet = call(
        functools.partial(pack_surface, rows_a, rows_o),
        0.8,
        4 << 20,
        in_specs=[HBM] * 7,
        out_specs=[VMEM] * 3 + [SMEM] * 2,
        out_shape=[
            pltpu.VMEM((block, SURF, lanes), BF16),
            pltpu.VMEM((1, channels_a), F32),
            pltpu.VMEM((1, channels_o), F32),
            pltpu.SMEM((2, pair_src.shape[1]), jnp.int32),
            pltpu.SMEM((1, rows_o), jnp.int32),
        ],
        scratch_shapes=[
            pltpu.VMEM((SURF * rows_a, lanes), F32),
            pltpu.VMEM((SURF * rows_o, lanes), F32),
            pltpu.SemaphoreType.DMA((7,)),
        ],
        name="pack_surface",
    )(
        hbm(atm),
        hbm(ocean),
        hbm(mask),
        hbm(pair_src),
        hbm(pair_tgt),
        hbm(atm_rate.reshape(1, channels_a)),
        hbm(ocean_rate.reshape(1, channels_o)),
    )
    received = exchange([surface] * len(routes), routes)

    halo = pltpu.VMEM((2, channels, lanes), BF16)
    even_rows, odd_rows, rate, live = call(
        functools.partial(prepare, rows_a, rows_o),
        0.5,
        4 << 20,
        in_specs=[VMEM, VMEM, SMEM, HBM, VMEM, VMEM],
        out_specs=[VMEM] * 3 + [SMEM],
        out_shape=[
            halo,
            halo,
            pltpu.VMEM((channels, lanes), F32),
            pltpu.SMEM((1, pair_src.shape[1]), jnp.int32),
        ],
        name="prepare",
    )(atm, ocean, pair_count, hbm(remap_weight[0]), rate_a, rate_o)
    even_in = lax.ppermute(even_rows, "comp", even_pairs)
    odd_in = lax.ppermute(odd_rows, "comp", odd_pairs)

    sends = [jax.ShapeDtypeStruct((message + extra, lanes), BF16)] * 2
    sends += [jax.ShapeDtypeStruct((message, lanes), BF16)] * (tile_count - 3)
    own_part, *parts = call(
        functools.partial(remap, tile_count, rows_a, rows_o),
        2.0,
        12 << 20,
        in_specs=[SMEM, SMEM] + [VMEM] * (1 + tile_count),
        out_specs=[VMEM] * tile_count,
        out_shape=[jax.ShapeDtypeStruct((block, SURF, lanes), F32)] + sends,
        scratch_shapes=[
            pltpu.VMEM((tile_count * block, SURF, lanes), BF16),
            pltpu.VMEM((tile_count * block, SURF, lanes), F32),
        ],
        name="remap",
    )(table, live, remap_weight[0], surface, *received)
    parts[:2] = call(
        functools.partial(pack_columns, rows_a, rows_o),
        1.2,
        8 << 20,
        in_specs=[VMEM] * 7,
        out_specs=[VMEM, VMEM],
        out_shape=sends[:2],
        input_output_aliases={5: 0, 6: 1},
        scratch_shapes=[
            pltpu.VMEM((channels_a * rows_a + channels_o * rows_o, lanes), F32),
            pltpu.VMEM((2, extra, lanes), F32),
        ],
        name="pack_columns",
    )(atm, ocean, rate, even_in, odd_in, *parts[:2])
    returned = exchange(parts, routes)

    atm_base, ocean_base = call(
        functools.partial(stencil, rows_a, rows_o),
        2.5,
        8 << 20,
        in_specs=[VMEM] * 5,
        out_specs=[VMEM, VMEM],
        out_shape=[
            jax.ShapeDtypeStruct(atm.shape, F32),
            jax.ShapeDtypeStruct(ocean.shape, F32),
        ],
        name="stencil",
    )(atm, ocean, rate, even_in, odd_in)

    atm_next, ocean_next = call(
        functools.partial(final, tile_count, rows_a, rows_o),
        2.0,
        12 << 20,
        in_specs=[SMEM] + [VMEM] * (2 + tile_count),
        out_specs=[HBM, HBM],
        out_shape=[
            jax.ShapeDtypeStruct(atm.shape, F32),
            jax.ShapeDtypeStruct(ocean.shape, F32),
        ],
        scratch_shapes=[
            pltpu.VMEM((SURF * block, lanes), F32),
            pltpu.VMEM(atm.shape, F32),
            pltpu.VMEM(ocean.shape, F32),
            pltpu.SemaphoreType.DMA((channels // 8,)),
        ],
        name="final",
    )(wet, atm_base, ocean_base, own_part, *returned)
    return (
        atm_next.reshape(channels_a, rows_a, lanes),
        ocean_next.reshape(channels_o, rows_o, lanes),
    )


def solution(mesh):
    return jax.shard_map(
        interval,
        mesh=mesh,
        in_specs=(
            P(None, "comp", "tile"),
            P(None, "comp", "tile"),
            P(),
            P(),
            P("comp", "tile"),
            P("comp", "tile", None, None),
            P("comp", "tile"),
            P("comp", "tile"),
            P("comp", "tile"),
        ),
        out_specs=(P(None, "comp", "tile"), P(None, "comp", "tile")),
        check_vma=False,
    )
```

```python
import functools

import jax
import jax.numpy as jnp
from jax import lax
from jax.experimental import pallas as pl
from jax.experimental.pallas import tpu as pltpu
from jax.sharding import PartitionSpec as P


SURF = 8
F32 = jnp.float32
BF16 = jnp.bfloat16
VMEM = pl.BlockSpec(memory_space=pltpu.VMEM)
SMEM = pl.BlockSpec(memory_space=pltpu.SMEM)
HBM = pl.BlockSpec(memory_space=pltpu.HBM)
ANY = pl.BlockSpec(memory_space=pl.ANY)


def beside_even(index):
    return index + 1 - 2 * (index % 2)


def beside_odd(index, count):
    return (index - 1 + 2 * (index % 2) + count) % count


def tile_pairs(count):
    routes = [
        [(i, beside_even(i)) for i in range(count)],
        [(i, beside_odd(i, count)) for i in range(count)],
    ]
    routes += [[(i, (i + s) % count) for i in range(count)] for s in range(2, count - 1)]
    return routes


def peers(me, count):
    a = beside_even(me)
    b = beside_odd(me, count)
    far = range(2, count - 1)
    sources = [a, b] + [lax.rem(me - s + count, count) for s in far]
    targets = [a, b] + [lax.rem(me + s, count) for s in far]
    return sources, targets


def comp_pairs(count):
    even = [(i, beside_even(i)) for i in range(count)]
    odd = [(i, beside_odd(i, count)) for i in range(count)]
    return even, odd


def pack_surface(rows_a, rows_o, *refs):
    atm_in, ocean_in, mask_in, src_in, tgt_in, rate_a_in, rate_o_in = refs[:7]
    surface, rate_a, rate_o, table, mask, atm, ocean, done = refs[7:]
    copies = [
        (mask_in, mask),
        (atm_in.at[0 : SURF * rows_a], atm),
        (ocean_in.at[0 : SURF * rows_o], ocean),
        (src_in, table.at[0:1]),
        (tgt_in, table.at[1:2]),
        (rate_a_in, rate_a),
        (rate_o_in, rate_o),
    ]
    copies = [pltpu.make_async_copy(a, b, done.at[i]) for i, (a, b) in enumerate(copies)]
    for copy in copies:
        copy.start()
    copies[1].wait()
    for y in range(rows_a):
        surface[y] = atm[pl.ds(y, SURF, stride=rows_a), :].astype(BF16)
    copies[0].wait()
    copies[2].wait()
    for y in range(rows_o):
        tile = ocean[pl.ds(y, SURF, stride=rows_o), :]
        surface[rows_a + y] = (tile * mask[0, y].astype(F32)).astype(BF16)
    for copy in copies[3:]:
        copy.wait()


def prepare(rows_a, rows_o, *refs):
    atm, ocean, number, _, rate_a, rate_o = refs[:6]
    even_out, odd_out, rate, live = refs[6:]
    live[0, 0] = number[0, 0]
    parity = lax.rem(lax.axis_index("comp"), 2)
    at = 0
    for ref, rows in ((atm, rows_a), (ocean, rows_o)):
        channels = ref.shape[0] // rows
        for c in range(0, channels, 8):
            for r in range(2):
                low = ref[pl.ds(c * rows + r, 8, stride=rows), :]
                high = ref[pl.ds(c * rows + rows - 2 + r, 8, stride=rows), :]
                even_out[r, at + c : at + c + 8, :] = jnp.where(parity == 0, high, low).astype(BF16)
                odd_out[r, at + c : at + c + 8, :] = jnp.where(parity == 0, low, high).astype(BF16)
        at += channels
    lanes = atm.shape[1]
    split = rate_a.shape[1]
    rate[0:split, :] = jnp.broadcast_to(rate_a[...], (lanes, split)).T
    rate[split:, :] = jnp.broadcast_to(rate_o[...], (lanes, rate_o.shape[1])).T


def halo_rows(comp, even_in, odd_in, at):
    parity = lax.rem(comp, 2)
    outside = (comp == 0) | (comp == lax.axis_size("comp") - 1)
    e = [even_in[r, at : at + 8, :].astype(F32) for r in range(2)]
    o = [odd_in[r, at : at + 8, :].astype(F32) for r in range(2)]
    o = [jnp.where(outside, jnp.zeros_like(x), x) for x in o]
    north = [jnp.where(parity == 0, o[r], e[r]) for r in range(2)]
    south = [jnp.where(parity == 0, e[r], o[r]) for r in range(2)]
    return north, south


def pack_columns(rows_a, rows_o, atm, ocean, rate, out, spread):
    tile_parity = lax.rem(lax.axis_index("tile"), 2)
    lanes = atm.shape[1]
    row = lax.broadcasted_iota(jnp.int32, (8, lanes), 0)
    lane = lax.broadcasted_iota(jnp.int32, (8, lanes), 1)
    east = lax.div(row, 2) == tile_parity
    second = lax.rem(row, 2)
    spot = jnp.where(east, lanes - 1 - second, second)
    pick = jnp.where((row < 4) & (lane == spot), 1.0, 0.0).astype(BF16)
    outer = (lane == 0) | (lane == lanes - 1)
    turn = (lane == 1) | (lane == lanes - 1)
    dims = (((1,), (1,)), ((), ()))
    out[...] = jnp.zeros_like(out)
    at = 0
    for ref, rows in ((atm, rows_a), (ocean, rows_o)):
        channels = ref.shape[0] // rows
        for c in range(0, channels, 8):
            rho = rate[at + c : at + c + 8, :]
            own = 2.0 * rho * (1.0 - 4.0 * rho)
            square = rho * rho
            q = [ref[pl.ds(c * rows + r, 8, stride=rows), :] for r in range(rows)]
            for r in range(rows):
                far = square * q[r]
                beside = q[1] if r == 0 else q[r - 1]
                if 0 < r < rows - 1:
                    beside = beside + q[r + 1]
                near = own * q[r] + 2.0 * square * beside
                moved = jnp.where(turn, pltpu.roll(far, 1, 1), pltpu.roll(far, lanes - 1, 1))
                value = moved + jnp.where(outer, near, 0.0)
                spread[pl.ds((at + c) * rows + r, 8, stride=rows), :] = value
        at += channels
    for j in range(at // 8):
        part = spread[j * 8 * rows_a : (j + 1) * 8 * rows_a, :].astype(BF16)
        found = lax.dot_general(pick, part, dims, preferred_element_type=F32)
        out[0, 2 * j : 2 * j + 2, :] = found[0:2, :]
        out[1, 2 * j : 2 * j + 2, :] = found[2:4, :]


def corners(stage, even_in, odd_in, part_a, part_b, out_a, out_b, joined):
    del part_a, part_b
    comp = lax.axis_index("comp")
    parity = lax.rem(comp, 2)
    outside = (comp == 0) | (comp == lax.axis_size("comp") - 1)
    tile_parity = lax.rem(lax.axis_index("tile"), 2)
    channels, lanes = even_in.shape[1:]
    row = lax.broadcasted_iota(jnp.int32, (8, lanes), 0)
    lane = lax.broadcasted_iota(jnp.int32, (8, lanes), 1)
    spot = jnp.where(row == tile_parity, lanes - 1, 0)
    pick = jnp.where((row < 2) & (lane == spot), 1.0, 0.0).astype(BF16)
    dims = (((1,), (1,)), ((), ()))
    joined[...] = stage[...]
    pieces = -(-channels // lanes)
    first = 2 * channels // 8
    for side in range(2):
        even = even_in[1 - side]
        odd = odd_in[1 - side]
        odd = jnp.where(outside, jnp.zeros_like(odd), odd)
        beyond = jnp.where(parity == side, odd, even)
        for i in range(pieces):
            part = beyond[i * lanes : min((i + 1) * lanes, channels), :]
            found = lax.dot_general(pick, part, dims, preferred_element_type=F32)
            at = first + side * pieces + i
            for k in range(2):
                joined[k, at : at + 1, 0 : part.shape[0]] = found[k : k + 1, :]
    behind = out_a.shape[0] - joined.shape[1]
    out_a[behind:, :] = joined[0].astype(BF16)
    out_b[behind:, :] = joined[1].astype(BF16)


def remap(tile_count, rows_a, rows_o, *refs):
    table, number, weights, own = refs[:4]
    got = refs[4 : 3 + tile_count]
    own_out = refs[3 + tile_count]
    outs = refs[4 + tile_count : 3 + 2 * tile_count]
    band, total = refs[3 + 2 * tile_count :]
    block = rows_a + rows_o
    me = lax.axis_index("tile")
    sources, targets = peers(me, tile_count)
    band[pl.ds(me * block, block)] = own[...]
    for e, ref in zip(sources, got):
        band[pl.ds(e * block, block)] = ref[...]
    total[...] = jnp.zeros_like(total)
    pairs = weights.shape[0]
    live_count = number[0, 0]
    trans = (((1,), (1,)), ((), ()))
    plain = (((1,), (0,)), ((), ()))
    group = 8
    for start in range(0, pairs, group):
        made = []
        for k in range(start, min(start + group, pairs)):
            a = table[0, k]
            o = table[1, k]
            at_a = lax.div(a, rows_a) * block + lax.rem(a, rows_a)
            at_o = lax.div(o, rows_o) * block + rows_a + lax.rem(o, rows_o)
            live = k < live_count
            w = weights[k]
            ta = band[at_a]
            to = band[at_o]
            ta = jnp.where(live, ta, jnp.zeros_like(ta))
            to = jnp.where(live, to, jnp.zeros_like(to))
            ahead = lax.dot_general(ta, w, plain, preferred_element_type=F32)
            back = lax.dot_general(to, w, trans, preferred_element_type=F32)
            made.append((at_a, at_o, ahead, back))
        for at_a, at_o, ahead, back in made:
            total[at_o] += ahead
            total[at_a] += back
    own_out[...] = total[pl.ds(me * block, block)]
    lanes = weights.shape[2]
    for e, ref in zip(targets, outs):
        part = total[pl.ds(e * block, block)].astype(BF16)
        ref[0 : block * SURF, :] = part.reshape(block * SURF, lanes)


def stencil(rows_a, rows_o, atm, ocean, rate, even_in, odd_in, atm_out, ocean_out):
    comp = lax.axis_index("comp")
    lanes = atm.shape[1]
    lane = lax.broadcasted_iota(jnp.int32, (8, lanes), 1)
    at_west = lane == 0
    at_east = lane == lanes - 1
    keep_north = jnp.where(comp == 0, 0.0, 1.0).astype(F32)
    keep_south = jnp.where(comp == lax.axis_size("comp") - 1, 0.0, 1.0).astype(F32)
    at = 0
    for ref, rows, out in ((atm, rows_a, atm_out), (ocean, rows_o, ocean_out)):
        channels = ref.shape[0] // rows
        for c in range(0, channels, 8):
            rho = rate[at + c : at + c + 8, :]
            own = 1.0 - 4.0 * rho
            north, south = halo_rows(comp, even_in, odd_in, at + c)
            q = north + [ref[pl.ds(c * rows + r, 8, stride=rows), :] for r in range(rows)] + south
            p = []
            for i in range(1, rows + 3):
                west = jnp.where(at_west, 0.0, pltpu.roll(q[i], 1, 1))
                east = jnp.where(at_east, 0.0, pltpu.roll(q[i], lanes - 1, 1))
                p.append(own * q[i] + rho * ((q[i - 1] + q[i + 1]) + (west + east)))
            p[0] = p[0] * keep_north
            p[rows + 1] = p[rows + 1] * keep_south
            for r in range(rows):
                ghost = rho * q[r + 2]
                west = jnp.where(at_west, ghost, pltpu.roll(p[r + 1], 1, 1))
                east = jnp.where(at_east, ghost, pltpu.roll(p[r + 1], lanes - 1, 1))
                out[pl.ds(c * rows + r, 8, stride=rows), :] = own * p[r + 1] + rho * (
                    (p[r] + p[r + 2]) + (west + east)
                )
        at += channels


def edges(rows_a, rows_o, mask, rate, atm, ocean, own, got_a, got_b, *refs):
    atm_out, ocean_out, surface, force, north, south, value_a, value_o, done = refs
    channels, lanes = rate.shape
    block = rows_a + rows_o
    message = block * SURF
    tile_parity = lax.rem(lax.axis_index("tile"), 2)
    row = lax.broadcasted_iota(jnp.int32, (8, lanes), 0)
    lane = lax.broadcasted_iota(jnp.int32, (8, lanes), 1)
    east = lax.div(row, 2) == tile_parity
    second = lax.rem(row, 2)
    spot = jnp.where(east, lanes - 1 - second, second)
    place = jnp.where((row < 4) & (lane == spot), 1.0, 0.0).astype(BF16)
    outer = jnp.where(row == tile_parity, lanes - 1, 0)
    place_outer = jnp.where((row < 2) & (lane == outer), 1.0, 0.0).astype(BF16)
    dims = (((0,), (0,)), ((), ()))

    def sides(at, count):
        rows = [got_a[at : at + count, :].astype(F32), got_b[at : at + count, :].astype(F32)]
        rows.append(jnp.zeros((8 - 2 * count, lanes), F32))
        return jnp.concatenate(rows, axis=0).astype(BF16)

    pieces = -(-channels // lanes)
    first = message + 2 * channels // 8
    for side, ref in ((0, north), (1, south)):
        for i in range(pieces):
            size = min(lanes, channels - i * lanes)
            cells = lax.dot_general(
                sides(first + side * pieces + i, 1), place_outer, dims, preferred_element_type=F32
            )
            rho = rate[i * lanes : i * lanes + size, :]
            ref[i * lanes : i * lanes + size, :] = 2.0 * rho * rho * cells[0:size, :]
    group = 32
    at = 0
    copies = []
    for ref, keep, out, rows in (
        (atm, value_a, atm_out, rows_a),
        (ocean, value_o, ocean_out, rows_o),
    ):
        count = ref.shape[0] // rows
        for c in range(0, count, 8):
            keep[c * rows : (c + 8) * rows, :] = ref[
                c * rows : (c + 8) * rows, :
            ] + lax.dot_general(
                sides(message + 2 * ((at + c) // 8), 2), place, dims, preferred_element_type=F32
            )
            top = pl.ds(c * rows, 8, stride=rows)
            bottom = pl.ds(c * rows + rows - 1, 8, stride=rows)
            keep[top, :] = keep[top, :] + north[at + c : at + c + 8, :]
            keep[bottom, :] = keep[bottom, :] + south[at + c : at + c + 8, :]
            if (c + 8) % group == 0 or c + 8 == count:
                begin = max(c // group * group, SURF) * rows
                end = (c + 8) * rows
                copies.append(
                    pltpu.make_async_copy(
                        keep.at[begin:end], out.at[begin:end], done.at[len(copies)]
                    )
                )
                copies[-1].start()
        at += count
    for y in range(block):
        total = own[y]
        for ref in (got_a, got_b):
            total = total + ref[SURF * y : SURF * y + SURF, :].astype(F32)
        if y >= rows_a:
            total = total * mask[0, y - rows_a].astype(F32)
        start = y if y < rows_a else SURF * rows_a + y - rows_a
        force[pl.ds(start, SURF, stride=rows_a if y < rows_a else rows_o), :] = total
    split = SURF * rows_a
    surface[0:split, :] = value_a[0:split, :] + force[0:split, :]
    surface[split:, :] = value_o[0 : SURF * rows_o, :] + force[split:, :]
    for copy in copies:
        copy.wait()


def final(rows_a, rows_o, mask, surface, *refs):
    got = refs[:-7]
    _, _, atm_out, ocean_out, force, value, done = refs[-7:]
    block = rows_a + rows_o
    for y in range(block):
        total = got[0][SURF * y : SURF * y + SURF, :].astype(F32)
        for ref in got[1:]:
            total = total + ref[SURF * y : SURF * y + SURF, :].astype(F32)
        if y >= rows_a:
            total = total * mask[0, y - rows_a].astype(F32)
        start = y if y < rows_a else SURF * rows_a + y - rows_a
        force[pl.ds(start, SURF, stride=rows_a if y < rows_a else rows_o), :] = total
    split = SURF * rows_a
    copies = []
    for i, (begin, end, out) in enumerate(
        ((0, split, atm_out), (split, SURF * block, ocean_out))
    ):
        value[begin:end, :] = surface[begin:end, :] + force[begin:end, :]
        copies.append(
            pltpu.make_async_copy(value.at[begin:end], out.at[0 : end - begin], done.at[i])
        )
        copies[-1].start()
    for copy in copies:
        copy.wait()


def call(body, micros, limit, **rest):
    return pl.pallas_call(
        body,
        compiler_params=pltpu.CompilerParams(vmem_limit_bytes=limit),
        cost_estimate=pl.CostEstimate(
            flops=0, transcendentals=0, bytes_accessed=int(micros * 3.0e6)
        ),
        **rest,
    )


def exchange(blocks, routes):
    out = []
    for block, route in zip(blocks, routes):
        out.append(lax.ppermute(block, "tile", route))
    return out


def interval(
    atm_state,
    ocean_state,
    atm_rate,
    ocean_rate,
    ocean_mask,
    remap_weight,
    pair_src,
    pair_tgt,
    pair_count,
):
    channels_a, rows_a, lanes = atm_state.shape
    channels_o, rows_o, _ = ocean_state.shape
    channels = channels_a + channels_o
    tile_count = lax.axis_size("tile")
    block = rows_a + rows_o
    message = block * SURF
    extra = -(-(2 * channels // 8 + 2 * -(-channels // lanes)) // 16) * 16
    atm = atm_state.reshape(channels_a * rows_a, lanes)
    ocean = ocean_state.reshape(channels_o * rows_o, lanes)
    mask = ocean_mask.reshape(1, rows_o)
    routes = tile_pairs(tile_count)
    even_pairs, odd_pairs = comp_pairs(lax.axis_size("comp"))

    hbm = lambda x: pltpu.with_memory_space_constraint(x, pltpu.HBM)
    surface, rate_a, rate_o, table, wet = call(
        functools.partial(pack_surface, rows_a, rows_o),
        0.8,
        4 << 20,
        in_specs=[HBM] * 7,
        out_specs=[VMEM] * 3 + [SMEM] * 2,
        out_shape=[
            pltpu.VMEM((block, SURF, lanes), BF16),
            pltpu.VMEM((1, channels_a), F32),
            pltpu.VMEM((1, channels_o), F32),
            pltpu.SMEM((2, pair_src.shape[1]), jnp.int32),
            pltpu.SMEM((1, rows_o), jnp.int32),
        ],
        scratch_shapes=[
            pltpu.VMEM((SURF * rows_a, lanes), F32),
            pltpu.VMEM((SURF * rows_o, lanes), F32),
            pltpu.SemaphoreType.DMA((7,)),
        ],
        name="pack_surface",
    )(
        hbm(atm),
        hbm(ocean),
        hbm(mask),
        hbm(pair_src),
        hbm(pair_tgt),
        hbm(atm_rate.reshape(1, channels_a)),
        hbm(ocean_rate.reshape(1, channels_o)),
    )
    received = exchange([surface] * len(routes), routes)

    halo = pltpu.VMEM((2, channels, lanes), BF16)
    even_rows, odd_rows, rate, live = call(
        functools.partial(prepare, rows_a, rows_o),
        0.5,
        4 << 20,
        in_specs=[VMEM, VMEM, SMEM, HBM, VMEM, VMEM],
        out_specs=[VMEM] * 3 + [SMEM],
        out_shape=[
            halo,
            halo,
            pltpu.VMEM((channels, lanes), F32),
            pltpu.SMEM((1, pair_src.shape[1]), jnp.int32),
        ],
        name="prepare",
    )(atm, ocean, pair_count, hbm(remap_weight[0]), rate_a, rate_o)
    even_in = lax.ppermute(even_rows, "comp", even_pairs)
    odd_in = lax.ppermute(odd_rows, "comp", odd_pairs)

    stage = call(
        functools.partial(pack_columns, rows_a, rows_o),
        1.1,
        8 << 20,
        in_specs=[VMEM] * 3,
        out_specs=VMEM,
        out_shape=pltpu.VMEM((2, extra, lanes), F32),
        scratch_shapes=[pltpu.VMEM((channels_a * rows_a + channels_o * rows_o, lanes), F32)],
        name="pack_columns",
    )(atm, ocean, rate)

    sends = [jax.ShapeDtypeStruct((message + extra, lanes), BF16)] * 2
    sends += [jax.ShapeDtypeStruct((message, lanes), BF16)] * (tile_count - 3)
    own_part, *parts = call(
        functools.partial(remap, tile_count, rows_a, rows_o),
        2.0,
        12 << 20,
        in_specs=[SMEM, SMEM] + [VMEM] * (1 + tile_count),
        out_specs=[VMEM] * tile_count,
        out_shape=[jax.ShapeDtypeStruct((block, SURF, lanes), F32)] + sends,
        scratch_shapes=[
            pltpu.VMEM((tile_count * block, SURF, lanes), BF16),
            pltpu.VMEM((tile_count * block, SURF, lanes), F32),
        ],
        name="remap",
    )(table, live, remap_weight[0], surface, *received)
    parts[:2] = call(
        corners,
        0.3,
        8 << 20,
        in_specs=[VMEM] * 5,
        out_specs=[VMEM, VMEM],
        out_shape=sends[:2],
        input_output_aliases={3: 0, 4: 1},
        scratch_shapes=[pltpu.VMEM((2, extra, lanes), F32)],
        name="corners",
    )(stage, even_in, odd_in, *parts[:2])
    returned = exchange(parts, routes)

    atm_base, ocean_base = call(
        functools.partial(stencil, rows_a, rows_o),
        2.5,
        8 << 20,
        in_specs=[VMEM] * 5,
        out_specs=[VMEM, VMEM],
        out_shape=[
            jax.ShapeDtypeStruct(atm.shape, F32),
            jax.ShapeDtypeStruct(ocean.shape, F32),
        ],
        name="stencil",
    )(atm, ocean, rate, even_in, odd_in)

    result = [pltpu.HBM(atm.shape, F32), pltpu.HBM(ocean.shape, F32)]
    atm_next, ocean_next, base = call(
        functools.partial(edges, rows_a, rows_o),
        1.5,
        12 << 20,
        in_specs=[SMEM] + [VMEM] * 6,
        out_specs=[HBM, HBM, VMEM],
        out_shape=result + [pltpu.VMEM((message, lanes), F32)],
        scratch_shapes=[
            pltpu.VMEM((message, lanes), F32),
            pltpu.VMEM((channels, lanes), F32),
            pltpu.VMEM((channels, lanes), F32),
            pltpu.VMEM(atm.shape, F32),
            pltpu.VMEM(ocean.shape, F32),
            pltpu.SemaphoreType.DMA((channels // 8,)),
        ],
        name="edges",
    )(wet, rate, atm_base, ocean_base, own_part, *returned[:2])
    far = returned[2:]
    atm_next, ocean_next = call(
        functools.partial(final, rows_a, rows_o),
        0.7,
        4 << 20,
        in_specs=[SMEM] + [VMEM] * (1 + len(far)) + [HBM, HBM],
        out_specs=[HBM, HBM],
        out_shape=result,
        input_output_aliases={2 + len(far): 0, 3 + len(far): 1},
        scratch_shapes=[
            pltpu.VMEM((message, lanes), F32),
            pltpu.VMEM((message, lanes), F32),
            pltpu.SemaphoreType.DMA((2,)),
        ],
        name="final",
    )(wet, base, *far, hbm(atm_next), hbm(ocean_next))
    return (
        atm_next.reshape(channels_a, rows_a, lanes),
        ocean_next.reshape(channels_o, rows_o, lanes),
    )


def solution(mesh):
    return jax.shard_map(
        interval,
        mesh=mesh,
        in_specs=(
            P(None, "comp", "tile"),
            P(None, "comp", "tile"),
            P(),
            P(),
            P("comp", "tile"),
            P("comp", "tile", None, None),
            P("comp", "tile"),
            P("comp", "tile"),
            P("comp", "tile"),
        ),
        out_specs=(P(None, "comp", "tile"), P(None, "comp", "tile")),
        check_vma=False,
    )
```

```python
import functools

import jax
import jax.numpy as jnp
from jax import lax
from jax.experimental import pallas as pl
from jax.experimental.pallas import tpu as pltpu
from jax.sharding import PartitionSpec as P


SURF = 8
F32 = jnp.float32
BF16 = jnp.bfloat16
VMEM = pl.BlockSpec(memory_space=pltpu.VMEM)
SMEM = pl.BlockSpec(memory_space=pltpu.SMEM)
HBM = pl.BlockSpec(memory_space=pltpu.HBM)
ANY = pl.BlockSpec(memory_space=pl.ANY)


def beside_even(index):
    return index + 1 - 2 * (index % 2)


def beside_odd(index, count):
    return (index - 1 + 2 * (index % 2) + count) % count


def tile_pairs(count):
    routes = [
        [(i, beside_even(i)) for i in range(count)],
        [(i, beside_odd(i, count)) for i in range(count)],
    ]
    routes += [[(i, (i + s) % count) for i in range(count)] for s in range(2, count - 1)]
    return routes


def peers(me, count):
    a = beside_even(me)
    b = beside_odd(me, count)
    far = range(2, count - 1)
    sources = [a, b] + [lax.rem(me - s + count, count) for s in far]
    targets = [a, b] + [lax.rem(me + s, count) for s in far]
    return sources, targets


def comp_pairs(count):
    even = [(i, beside_even(i)) for i in range(count)]
    odd = [(i, beside_odd(i, count)) for i in range(count)]
    return even, odd


def pack_surface(rows_a, rows_o, *refs):
    atm_in, ocean_in, mask_in, src_in, tgt_in, rate_a_in, rate_o_in = refs[:7]
    surface, rate_a, rate_o, table, mask, atm, ocean, done = refs[7:]
    copies = [
        (mask_in, mask),
        (atm_in.at[0 : SURF * rows_a], atm),
        (ocean_in.at[0 : SURF * rows_o], ocean),
        (src_in, table.at[0:1]),
        (tgt_in, table.at[1:2]),
        (rate_a_in, rate_a),
        (rate_o_in, rate_o),
    ]
    copies = [pltpu.make_async_copy(a, b, done.at[i]) for i, (a, b) in enumerate(copies)]
    for copy in copies:
        copy.start()
    copies[1].wait()
    for y in range(rows_a):
        surface[y] = atm[pl.ds(y, SURF, stride=rows_a), :].astype(BF16)
    copies[0].wait()
    copies[2].wait()
    for y in range(rows_o):
        tile = ocean[pl.ds(y, SURF, stride=rows_o), :]
        surface[rows_a + y] = (tile * mask[0, y].astype(F32)).astype(BF16)
    for copy in copies[3:]:
        copy.wait()


def prepare(rows_a, rows_o, *refs):
    atm, ocean, number, _, rate_a, rate_o = refs[:6]
    even_out, odd_out, rate, live = refs[6:]
    live[0, 0] = number[0, 0]
    parity = lax.rem(lax.axis_index("comp"), 2)
    at = 0
    for ref, rows in ((atm, rows_a), (ocean, rows_o)):
        channels = ref.shape[0] // rows
        for c in range(0, channels, 8):
            for r in range(2):
                low = ref[pl.ds(c * rows + r, 8, stride=rows), :]
                high = ref[pl.ds(c * rows + rows - 2 + r, 8, stride=rows), :]
                even_out[r, at + c : at + c + 8, :] = jnp.where(parity == 0, high, low).astype(BF16)
                odd_out[r, at + c : at + c + 8, :] = jnp.where(parity == 0, low, high).astype(BF16)
        at += channels
    lanes = atm.shape[1]
    split = rate_a.shape[1]
    rate[0:split, :] = jnp.broadcast_to(rate_a[...], (lanes, split)).T
    rate[split:, :] = jnp.broadcast_to(rate_o[...], (lanes, rate_o.shape[1])).T


def halo_rows(comp, even_in, odd_in, at):
    parity = lax.rem(comp, 2)
    outside = (comp == 0) | (comp == lax.axis_size("comp") - 1)
    e = [even_in[r, at : at + 8, :].astype(F32) for r in range(2)]
    o = [odd_in[r, at : at + 8, :].astype(F32) for r in range(2)]
    o = [jnp.where(outside, jnp.zeros_like(x), x) for x in o]
    north = [jnp.where(parity == 0, o[r], e[r]) for r in range(2)]
    south = [jnp.where(parity == 0, e[r], o[r]) for r in range(2)]
    return north, south


def pack_columns(rows_a, rows_o, atm, ocean, rate, out, spread):
    tile_parity = lax.rem(lax.axis_index("tile"), 2)
    lanes = atm.shape[1]
    row = lax.broadcasted_iota(jnp.int32, (8, lanes), 0)
    lane = lax.broadcasted_iota(jnp.int32, (8, lanes), 1)
    east = lax.div(row, 2) == tile_parity
    second = lax.rem(row, 2)
    spot = jnp.where(east, lanes - 1 - second, second)
    pick = jnp.where((row < 4) & (lane == spot), 1.0, 0.0).astype(BF16)
    outer = (lane == 0) | (lane == lanes - 1)
    turn = (lane == 1) | (lane == lanes - 1)
    dims = (((1,), (1,)), ((), ()))
    out[...] = jnp.zeros_like(out)
    at = 0
    for ref, rows in ((atm, rows_a), (ocean, rows_o)):
        channels = ref.shape[0] // rows
        for c in range(0, channels, 8):
            rho = rate[at + c : at + c + 8, :]
            own = 2.0 * rho * (1.0 - 4.0 * rho)
            square = rho * rho
            q = [ref[pl.ds(c * rows + r, 8, stride=rows), :] for r in range(rows)]
            for r in range(rows):
                far = square * q[r]
                beside = q[1] if r == 0 else q[r - 1]
                if 0 < r < rows - 1:
                    beside = beside + q[r + 1]
                near = own * q[r] + 2.0 * square * beside
                moved = jnp.where(turn, pltpu.roll(far, 1, 1), pltpu.roll(far, lanes - 1, 1))
                value = moved + jnp.where(outer, near, 0.0)
                spread[pl.ds((at + c) * rows + r, 8, stride=rows), :] = value
        at += channels
    for j in range(at // 8):
        part = spread[j * 8 * rows_a : (j + 1) * 8 * rows_a, :].astype(BF16)
        found = lax.dot_general(pick, part, dims, preferred_element_type=F32)
        out[0, 2 * j : 2 * j + 2, :] = found[0:2, :]
        out[1, 2 * j : 2 * j + 2, :] = found[2:4, :]


def corners(stage, even_in, odd_in, part_a, part_b, out_a, out_b, joined):
    del part_a, part_b
    comp = lax.axis_index("comp")
    parity = lax.rem(comp, 2)
    outside = (comp == 0) | (comp == lax.axis_size("comp") - 1)
    tile_parity = lax.rem(lax.axis_index("tile"), 2)
    channels, lanes = even_in.shape[1:]
    row = lax.broadcasted_iota(jnp.int32, (8, lanes), 0)
    lane = lax.broadcasted_iota(jnp.int32, (8, lanes), 1)
    spot = jnp.where(row == tile_parity, lanes - 1, 0)
    pick = jnp.where((row < 2) & (lane == spot), 1.0, 0.0).astype(BF16)
    dims = (((1,), (1,)), ((), ()))
    joined[...] = stage[...]
    pieces = -(-channels // lanes)
    first = 2 * channels // 8
    for side in range(2):
        even = even_in[1 - side]
        odd = odd_in[1 - side]
        odd = jnp.where(outside, jnp.zeros_like(odd), odd)
        beyond = jnp.where(parity == side, odd, even)
        for i in range(pieces):
            part = beyond[i * lanes : min((i + 1) * lanes, channels), :]
            found = lax.dot_general(pick, part, dims, preferred_element_type=F32)
            at = first + side * pieces + i
            for k in range(2):
                joined[k, at : at + 1, 0 : part.shape[0]] = found[k : k + 1, :]
    behind = out_a.shape[0] - joined.shape[1]
    out_a[behind:, :] = joined[0].astype(BF16)
    out_b[behind:, :] = joined[1].astype(BF16)


def remap(tile_count, rows_a, rows_o, *refs):
    table, number, weights, own = refs[:4]
    got = refs[4 : 3 + tile_count]
    own_out = refs[3 + tile_count]
    outs = refs[4 + tile_count : 3 + 2 * tile_count]
    band, total = refs[3 + 2 * tile_count :]
    block = rows_a + rows_o
    me = lax.axis_index("tile")
    sources, targets = peers(me, tile_count)
    band[pl.ds(me * block, block)] = own[...]
    for e, ref in zip(sources, got):
        band[pl.ds(e * block, block)] = ref[...]
    total[...] = jnp.zeros_like(total)
    pairs = weights.shape[0]
    live_count = number[0, 0]
    trans = (((1,), (1,)), ((), ()))
    plain = (((1,), (0,)), ((), ()))
    depth, width = weights.shape[1:]

    def picked(k):
        a = table[0, k]
        o = table[1, k]
        at_a = lax.div(a, rows_a) * block + lax.rem(a, rows_a)
        at_o = lax.div(o, rows_o) * block + rows_a + lax.rem(o, rows_o)
        live = k < live_count
        ta = band[at_a]
        to = band[at_o]
        ta = jnp.where(live, ta, jnp.zeros_like(ta))
        to = jnp.where(live, to, jnp.zeros_like(to))
        return at_a, at_o, ta, to

    for k in range(0, pairs, 2):
        first, second = picked(k), picked(k + 1)
        both = weights[k : k + 2].reshape(2 * depth, width)
        none = jnp.zeros_like(first[2])
        left = jnp.concatenate([first[2], none], axis=0)
        right = jnp.concatenate([none, second[2]], axis=0)
        ahead = lax.dot_general(
            jnp.concatenate([left, right], axis=1), both, plain, preferred_element_type=F32
        )
        back = lax.dot_general(
            jnp.concatenate([first[3], second[3]], axis=0), both, trans, preferred_element_type=F32
        )
        total[first[1]] += ahead[0:SURF]
        total[second[1]] += ahead[SURF:]
        total[first[0]] += back[0:SURF, 0:depth]
        total[second[0]] += back[SURF:, depth:]
    own_out[...] = total[pl.ds(me * block, block)]
    lanes = weights.shape[2]
    for e, ref in zip(targets, outs):
        part = total[pl.ds(e * block, block)].astype(BF16)
        ref[0 : block * SURF, :] = part.reshape(block * SURF, lanes)


def stencil(rows_a, rows_o, atm, ocean, rate, even_in, odd_in, atm_out, ocean_out):
    comp = lax.axis_index("comp")
    lanes = atm.shape[1]
    lane = lax.broadcasted_iota(jnp.int32, (8, lanes), 1)
    at_west = lane == 0
    at_east = lane == lanes - 1
    keep_north = jnp.where(comp == 0, 0.0, 1.0).astype(F32)
    keep_south = jnp.where(comp == lax.axis_size("comp") - 1, 0.0, 1.0).astype(F32)
    at = 0
    for ref, rows, out in ((atm, rows_a, atm_out), (ocean, rows_o, ocean_out)):
        channels = ref.shape[0] // rows
        for c in range(0, channels, 8):
            rho = rate[at + c : at + c + 8, :]
            own = 1.0 - 4.0 * rho
            north, south = halo_rows(comp, even_in, odd_in, at + c)
            q = north + [ref[pl.ds(c * rows + r, 8, stride=rows), :] for r in range(rows)] + south
            p = []
            for i in range(1, rows + 3):
                west = jnp.where(at_west, 0.0, pltpu.roll(q[i], 1, 1))
                east = jnp.where(at_east, 0.0, pltpu.roll(q[i], lanes - 1, 1))
                p.append(own * q[i] + rho * ((q[i - 1] + q[i + 1]) + (west + east)))
            p[0] = p[0] * keep_north
            p[rows + 1] = p[rows + 1] * keep_south
            for r in range(rows):
                ghost = rho * q[r + 2]
                west = jnp.where(at_west, ghost, pltpu.roll(p[r + 1], 1, 1))
                east = jnp.where(at_east, ghost, pltpu.roll(p[r + 1], lanes - 1, 1))
                out[pl.ds(c * rows + r, 8, stride=rows), :] = own * p[r + 1] + rho * (
                    (p[r] + p[r + 2]) + (west + east)
                )
        at += channels


def edges(rows_a, rows_o, mask, rate, atm, ocean, own, got_a, got_b, *refs):
    atm_out, ocean_out, surface, force, north, south, value_a, value_o, done = refs
    channels, lanes = rate.shape
    block = rows_a + rows_o
    message = block * SURF
    tile_parity = lax.rem(lax.axis_index("tile"), 2)
    row = lax.broadcasted_iota(jnp.int32, (8, lanes), 0)
    lane = lax.broadcasted_iota(jnp.int32, (8, lanes), 1)
    east = lax.div(row, 2) == tile_parity
    second = lax.rem(row, 2)
    spot = jnp.where(east, lanes - 1 - second, second)
    place = jnp.where((row < 4) & (lane == spot), 1.0, 0.0).astype(BF16)
    outer = jnp.where(row == tile_parity, lanes - 1, 0)
    place_outer = jnp.where((row < 2) & (lane == outer), 1.0, 0.0).astype(BF16)
    dims = (((0,), (0,)), ((), ()))

    def sides(at, count):
        rows = [got_a[at : at + count, :].astype(F32), got_b[at : at + count, :].astype(F32)]
        rows.append(jnp.zeros((8 - 2 * count, lanes), F32))
        return jnp.concatenate(rows, axis=0).astype(BF16)

    pieces = -(-channels // lanes)
    first = message + 2 * channels // 8
    for side, ref in ((0, north), (1, south)):
        for i in range(pieces):
            size = min(lanes, channels - i * lanes)
            cells = lax.dot_general(
                sides(first + side * pieces + i, 1), place_outer, dims, preferred_element_type=F32
            )
            rho = rate[i * lanes : i * lanes + size, :]
            ref[i * lanes : i * lanes + size, :] = 2.0 * rho * rho * cells[0:size, :]
    group = 32
    at = 0
    copies = []
    for ref, keep, out, rows in (
        (atm, value_a, atm_out, rows_a),
        (ocean, value_o, ocean_out, rows_o),
    ):
        count = ref.shape[0] // rows
        for c in range(0, count, 8):
            keep[c * rows : (c + 8) * rows, :] = ref[
                c * rows : (c + 8) * rows, :
            ] + lax.dot_general(
                sides(message + 2 * ((at + c) // 8), 2), place, dims, preferred_element_type=F32
            )
            top = pl.ds(c * rows, 8, stride=rows)
            bottom = pl.ds(c * rows + rows - 1, 8, stride=rows)
            keep[top, :] = keep[top, :] + north[at + c : at + c + 8, :]
            keep[bottom, :] = keep[bottom, :] + south[at + c : at + c + 8, :]
            if (c + 8) % group == 0 or c + 8 == count:
                begin = max(c // group * group, SURF) * rows
                end = (c + 8) * rows
                copies.append(
                    pltpu.make_async_copy(
                        keep.at[begin:end], out.at[begin:end], done.at[len(copies)]
                    )
                )
                copies[-1].start()
        at += count
    for y in range(block):
        total = own[y]
        for ref in (got_a, got_b):
            total = total + ref[SURF * y : SURF * y + SURF, :].astype(F32)
        if y >= rows_a:
            total = total * mask[0, y - rows_a].astype(F32)
        start = y if y < rows_a else SURF * rows_a + y - rows_a
        force[pl.ds(start, SURF, stride=rows_a if y < rows_a else rows_o), :] = total
    split = SURF * rows_a
    surface[0:split, :] = value_a[0:split, :] + force[0:split, :]
    surface[split:, :] = value_o[0 : SURF * rows_o, :] + force[split:, :]
    for copy in copies:
        copy.wait()


def final(rows_a, rows_o, mask, surface, *refs):
    got = refs[:-7]
    _, _, atm_out, ocean_out, force, value, done = refs[-7:]
    block = rows_a + rows_o
    for y in range(block):
        total = got[0][SURF * y : SURF * y + SURF, :].astype(F32)
        for ref in got[1:]:
            total = total + ref[SURF * y : SURF * y + SURF, :].astype(F32)
        if y >= rows_a:
            total = total * mask[0, y - rows_a].astype(F32)
        start = y if y < rows_a else SURF * rows_a + y - rows_a
        force[pl.ds(start, SURF, stride=rows_a if y < rows_a else rows_o), :] = total
    split = SURF * rows_a
    copies = []
    for i, (begin, end, out) in enumerate(
        ((0, split, atm_out), (split, SURF * block, ocean_out))
    ):
        value[begin:end, :] = surface[begin:end, :] + force[begin:end, :]
        copies.append(
            pltpu.make_async_copy(value.at[begin:end], out.at[0 : end - begin], done.at[i])
        )
        copies[-1].start()
    for copy in copies:
        copy.wait()


def call(body, micros, limit, **rest):
    return pl.pallas_call(
        body,
        compiler_params=pltpu.CompilerParams(vmem_limit_bytes=limit),
        cost_estimate=pl.CostEstimate(
            flops=0, transcendentals=0, bytes_accessed=int(micros * 3.0e6)
        ),
        **rest,
    )


def exchange(blocks, routes):
    out = []
    for block, route in zip(blocks, routes):
        out.append(lax.ppermute(block, "tile", route))
    return out


def interval(
    atm_state,
    ocean_state,
    atm_rate,
    ocean_rate,
    ocean_mask,
    remap_weight,
    pair_src,
    pair_tgt,
    pair_count,
):
    channels_a, rows_a, lanes = atm_state.shape
    channels_o, rows_o, _ = ocean_state.shape
    channels = channels_a + channels_o
    tile_count = lax.axis_size("tile")
    block = rows_a + rows_o
    message = block * SURF
    extra = -(-(2 * channels // 8 + 2 * -(-channels // lanes)) // 16) * 16
    atm = atm_state.reshape(channels_a * rows_a, lanes)
    ocean = ocean_state.reshape(channels_o * rows_o, lanes)
    mask = ocean_mask.reshape(1, rows_o)
    routes = tile_pairs(tile_count)
    even_pairs, odd_pairs = comp_pairs(lax.axis_size("comp"))

    hbm = lambda x: pltpu.with_memory_space_constraint(x, pltpu.HBM)
    surface, rate_a, rate_o, table, wet = call(
        functools.partial(pack_surface, rows_a, rows_o),
        0.8,
        4 << 20,
        in_specs=[HBM] * 7,
        out_specs=[VMEM] * 3 + [SMEM] * 2,
        out_shape=[
            pltpu.VMEM((block, SURF, lanes), BF16),
            pltpu.VMEM((1, channels_a), F32),
            pltpu.VMEM((1, channels_o), F32),
            pltpu.SMEM((2, pair_src.shape[1]), jnp.int32),
            pltpu.SMEM((1, rows_o), jnp.int32),
        ],
        scratch_shapes=[
            pltpu.VMEM((SURF * rows_a, lanes), F32),
            pltpu.VMEM((SURF * rows_o, lanes), F32),
            pltpu.SemaphoreType.DMA((7,)),
        ],
        name="pack_surface",
    )(
        hbm(atm),
        hbm(ocean),
        hbm(mask),
        hbm(pair_src),
        hbm(pair_tgt),
        hbm(atm_rate.reshape(1, channels_a)),
        hbm(ocean_rate.reshape(1, channels_o)),
    )
    received = exchange([surface] * len(routes), routes)

    halo = pltpu.VMEM((2, channels, lanes), BF16)
    even_rows, odd_rows, rate, live = call(
        functools.partial(prepare, rows_a, rows_o),
        0.5,
        4 << 20,
        in_specs=[VMEM, VMEM, SMEM, HBM, VMEM, VMEM],
        out_specs=[VMEM] * 3 + [SMEM],
        out_shape=[
            halo,
            halo,
            pltpu.VMEM((channels, lanes), F32),
            pltpu.SMEM((1, pair_src.shape[1]), jnp.int32),
        ],
        name="prepare",
    )(atm, ocean, pair_count, hbm(remap_weight[0]), rate_a, rate_o)
    even_in = lax.ppermute(even_rows, "comp", even_pairs)
    odd_in = lax.ppermute(odd_rows, "comp", odd_pairs)

    stage = call(
        functools.partial(pack_columns, rows_a, rows_o),
        1.1,
        8 << 20,
        in_specs=[VMEM] * 3,
        out_specs=VMEM,
        out_shape=pltpu.VMEM((2, extra, lanes), F32),
        scratch_shapes=[pltpu.VMEM((channels_a * rows_a + channels_o * rows_o, lanes), F32)],
        name="pack_columns",
    )(atm, ocean, rate)

    sends = [jax.ShapeDtypeStruct((message + extra, lanes), BF16)] * 2
    sends += [jax.ShapeDtypeStruct((message, lanes), BF16)] * (tile_count - 3)
    own_part, *parts = call(
        functools.partial(remap, tile_count, rows_a, rows_o),
        2.0,
        12 << 20,
        in_specs=[SMEM, SMEM] + [VMEM] * (1 + tile_count),
        out_specs=[VMEM] * tile_count,
        out_shape=[jax.ShapeDtypeStruct((block, SURF, lanes), F32)] + sends,
        scratch_shapes=[
            pltpu.VMEM((tile_count * block, SURF, lanes), BF16),
            pltpu.VMEM((tile_count * block, SURF, lanes), F32),
        ],
        name="remap",
    )(table, live, remap_weight[0], surface, *received)
    parts[:2] = call(
        corners,
        0.3,
        8 << 20,
        in_specs=[VMEM] * 5,
        out_specs=[VMEM, VMEM],
        out_shape=sends[:2],
        input_output_aliases={3: 0, 4: 1},
        scratch_shapes=[pltpu.VMEM((2, extra, lanes), F32)],
        name="corners",
    )(stage, even_in, odd_in, *parts[:2])
    returned = exchange(parts, routes)

    atm_base, ocean_base = call(
        functools.partial(stencil, rows_a, rows_o),
        2.5,
        8 << 20,
        in_specs=[VMEM] * 5,
        out_specs=[VMEM, VMEM],
        out_shape=[
            jax.ShapeDtypeStruct(atm.shape, F32),
            jax.ShapeDtypeStruct(ocean.shape, F32),
        ],
        name="stencil",
    )(atm, ocean, rate, even_in, odd_in)

    result = [pltpu.HBM(atm.shape, F32), pltpu.HBM(ocean.shape, F32)]
    atm_next, ocean_next, base = call(
        functools.partial(edges, rows_a, rows_o),
        1.5,
        12 << 20,
        in_specs=[SMEM] + [VMEM] * 6,
        out_specs=[HBM, HBM, VMEM],
        out_shape=result + [pltpu.VMEM((message, lanes), F32)],
        scratch_shapes=[
            pltpu.VMEM((message, lanes), F32),
            pltpu.VMEM((channels, lanes), F32),
            pltpu.VMEM((channels, lanes), F32),
            pltpu.VMEM(atm.shape, F32),
            pltpu.VMEM(ocean.shape, F32),
            pltpu.SemaphoreType.DMA((channels // 8,)),
        ],
        name="edges",
    )(wet, rate, atm_base, ocean_base, own_part, *returned[:2])
    far = returned[2:]
    atm_next, ocean_next = call(
        functools.partial(final, rows_a, rows_o),
        0.7,
        4 << 20,
        in_specs=[SMEM] + [VMEM] * (1 + len(far)) + [HBM, HBM],
        out_specs=[HBM, HBM],
        out_shape=result,
        input_output_aliases={2 + len(far): 0, 3 + len(far): 1},
        scratch_shapes=[
            pltpu.VMEM((message, lanes), F32),
            pltpu.VMEM((message, lanes), F32),
            pltpu.SemaphoreType.DMA((2,)),
        ],
        name="final",
    )(wet, base, *far, hbm(atm_next), hbm(ocean_next))
    return (
        atm_next.reshape(channels_a, rows_a, lanes),
        ocean_next.reshape(channels_o, rows_o, lanes),
    )


def solution(mesh):
    return jax.shard_map(
        interval,
        mesh=mesh,
        in_specs=(
            P(None, "comp", "tile"),
            P(None, "comp", "tile"),
            P(),
            P(),
            P("comp", "tile"),
            P("comp", "tile", None, None),
            P("comp", "tile"),
            P("comp", "tile"),
            P("comp", "tile"),
        ),
        out_specs=(P(None, "comp", "tile"), P(None, "comp", "tile")),
        check_vma=False,
    )
```

```python
import functools

import jax
import jax.numpy as jnp
from jax import lax
from jax.experimental import pallas as pl
from jax.experimental.pallas import tpu as pltpu
from jax.sharding import PartitionSpec as P


SURF = 8
F32 = jnp.float32
BF16 = jnp.bfloat16
VMEM = pl.BlockSpec(memory_space=pltpu.VMEM)
SMEM = pl.BlockSpec(memory_space=pltpu.SMEM)
HBM = pl.BlockSpec(memory_space=pltpu.HBM)
ANY = pl.BlockSpec(memory_space=pl.ANY)


def beside_even(index):
    return index + 1 - 2 * (index % 2)


def beside_odd(index, count):
    return (index - 1 + 2 * (index % 2) + count) % count


def tile_pairs(count):
    routes = [
        [(i, beside_even(i)) for i in range(count)],
        [(i, beside_odd(i, count)) for i in range(count)],
    ]
    routes += [[(i, (i + s) % count) for i in range(count)] for s in range(2, count - 1)]
    return routes


def peers(me, count):
    a = beside_even(me)
    b = beside_odd(me, count)
    far = range(2, count - 1)
    sources = [a, b] + [lax.rem(me - s + count, count) for s in far]
    targets = [a, b] + [lax.rem(me + s, count) for s in far]
    return sources, targets


def comp_pairs(count):
    even = [(i, beside_even(i)) for i in range(count)]
    odd = [(i, beside_odd(i, count)) for i in range(count)]
    return even, odd


def pack_surface(rows_a, rows_o, *refs):
    atm_in, ocean_in, mask_in, src_in, tgt_in, rate_a_in, rate_o_in = refs[:7]
    surface, rate_a, rate_o, table, mask, atm, ocean, done = refs[7:]
    copies = [
        (mask_in, mask),
        (atm_in.at[0 : SURF * rows_a], atm),
        (ocean_in.at[0 : SURF * rows_o], ocean),
        (src_in, table.at[0:1]),
        (tgt_in, table.at[1:2]),
        (rate_a_in, rate_a),
        (rate_o_in, rate_o),
    ]
    copies = [pltpu.make_async_copy(a, b, done.at[i]) for i, (a, b) in enumerate(copies)]
    for copy in copies:
        copy.start()
    copies[1].wait()
    for y in range(rows_a):
        surface[y] = atm[pl.ds(y, SURF, stride=rows_a), :].astype(BF16)
    copies[0].wait()
    copies[2].wait()
    for y in range(rows_o):
        tile = ocean[pl.ds(y, SURF, stride=rows_o), :]
        surface[rows_a + y] = (tile * mask[0, y].astype(F32)).astype(BF16)
    for copy in copies[3:]:
        copy.wait()


def prepare(rows_a, rows_o, *refs):
    atm, ocean, number, _, rate_a, rate_o = refs[:6]
    even_out, odd_out, rate, live = refs[6:]
    live[0, 0] = number[0, 0]
    parity = lax.rem(lax.axis_index("comp"), 2)
    at = 0
    for ref, rows in ((atm, rows_a), (ocean, rows_o)):
        channels = ref.shape[0] // rows
        for c in range(0, channels, 8):
            for r in range(2):
                low = ref[pl.ds(c * rows + r, 8, stride=rows), :]
                high = ref[pl.ds(c * rows + rows - 2 + r, 8, stride=rows), :]
                even_out[r, at + c : at + c + 8, :] = jnp.where(parity == 0, high, low).astype(BF16)
                odd_out[r, at + c : at + c + 8, :] = jnp.where(parity == 0, low, high).astype(BF16)
        at += channels
    lanes = atm.shape[1]
    split = rate_a.shape[1]
    rate[0:split, :] = jnp.broadcast_to(rate_a[...], (lanes, split)).T
    rate[split:, :] = jnp.broadcast_to(rate_o[...], (lanes, rate_o.shape[1])).T


def halo_rows(comp, even_in, odd_in, at):
    parity = lax.rem(comp, 2)
    outside = (comp == 0) | (comp == lax.axis_size("comp") - 1)
    e = [even_in[r, at : at + 8, :].astype(F32) for r in range(2)]
    o = [odd_in[r, at : at + 8, :].astype(F32) for r in range(2)]
    o = [jnp.where(outside, jnp.zeros_like(x), x) for x in o]
    north = [jnp.where(parity == 0, o[r], e[r]) for r in range(2)]
    south = [jnp.where(parity == 0, e[r], o[r]) for r in range(2)]
    return north, south


def pack_columns(rows_a, rows_o, atm, ocean, rate, out, lined, spread):
    tile_parity = lax.rem(lax.axis_index("tile"), 2)
    lanes = atm.shape[1]
    row = lax.broadcasted_iota(jnp.int32, (8, lanes), 0)
    lane = lax.broadcasted_iota(jnp.int32, (8, lanes), 1)
    east = lax.div(row, 2) == tile_parity
    second = lax.rem(row, 2)
    spot = jnp.where(east, lanes - 1 - second, second)
    pick = jnp.where((row < 4) & (lane == spot), 1.0, 0.0).astype(BF16)
    outer = (lane == 0) | (lane == lanes - 1)
    turn = (lane == 1) | (lane == lanes - 1)
    dims = (((1,), (1,)), ((), ()))
    out[...] = jnp.zeros_like(out)
    at = 0
    for ref, rows in ((atm, rows_a), (ocean, rows_o)):
        channels = ref.shape[0] // rows
        for c in range(0, channels, 8):
            rho = rate[at + c : at + c + 8, :]
            own = 2.0 * rho * (1.0 - 4.0 * rho)
            square = rho * rho
            q = [ref[pl.ds(c * rows + r, 8, stride=rows), :] for r in range(rows)]
            for r in range(rows):
                lined[r, at + c : at + c + 8, :] = q[r]
                far = square * q[r]
                beside = q[1] if r == 0 else q[r - 1]
                if 0 < r < rows - 1:
                    beside = beside + q[r + 1]
                near = own * q[r] + 2.0 * square * beside
                moved = jnp.where(turn, pltpu.roll(far, 1, 1), pltpu.roll(far, lanes - 1, 1))
                value = moved + jnp.where(outer, near, 0.0)
                spread[pl.ds((at + c) * rows + r, 8, stride=rows), :] = value
        at += channels
    for j in range(at // 8):
        part = spread[j * 8 * rows_a : (j + 1) * 8 * rows_a, :].astype(BF16)
        found = lax.dot_general(pick, part, dims, preferred_element_type=F32)
        out[0, 2 * j : 2 * j + 2, :] = found[0:2, :]
        out[1, 2 * j : 2 * j + 2, :] = found[2:4, :]


def corners(stage, even_in, odd_in, part_a, part_b, out_a, out_b, joined):
    del part_a, part_b
    comp = lax.axis_index("comp")
    parity = lax.rem(comp, 2)
    outside = (comp == 0) | (comp == lax.axis_size("comp") - 1)
    tile_parity = lax.rem(lax.axis_index("tile"), 2)
    channels, lanes = even_in.shape[1:]
    row = lax.broadcasted_iota(jnp.int32, (8, lanes), 0)
    lane = lax.broadcasted_iota(jnp.int32, (8, lanes), 1)
    spot = jnp.where(row == tile_parity, lanes - 1, 0)
    pick = jnp.where((row < 2) & (lane == spot), 1.0, 0.0).astype(BF16)
    dims = (((1,), (1,)), ((), ()))
    joined[...] = stage[...]
    pieces = -(-channels // lanes)
    first = 2 * channels // 8
    for side in range(2):
        even = even_in[1 - side]
        odd = odd_in[1 - side]
        odd = jnp.where(outside, jnp.zeros_like(odd), odd)
        beyond = jnp.where(parity == side, odd, even)
        for i in range(pieces):
            part = beyond[i * lanes : min((i + 1) * lanes, channels), :]
            found = lax.dot_general(pick, part, dims, preferred_element_type=F32)
            at = first + side * pieces + i
            for k in range(2):
                joined[k, at : at + 1, 0 : part.shape[0]] = found[k : k + 1, :]
    behind = out_a.shape[0] - joined.shape[1]
    out_a[behind:, :] = joined[0].astype(BF16)
    out_b[behind:, :] = joined[1].astype(BF16)


def quotient(number, divisor):
    if divisor & (divisor - 1) == 0:
        return lax.shift_right_logical(number, divisor.bit_length() - 1)
    return lax.div(number, divisor)


def remap(tile_count, rows_a, rows_o, *refs):
    table, number, weights, own = refs[:4]
    got = refs[4 : 3 + tile_count]
    own_out = refs[3 + tile_count]
    outs = refs[4 + tile_count : 3 + 2 * tile_count]
    band, total = refs[3 + 2 * tile_count :]
    block = rows_a + rows_o
    me = lax.axis_index("tile")
    sources, targets = peers(me, tile_count)
    band[pl.ds(me * block, block)] = own[...]
    for e, ref in zip(sources, got):
        band[pl.ds(e * block, block)] = ref[...]
    total[...] = jnp.zeros_like(total)
    pairs = weights.shape[0]
    live_count = number[0, 0]
    trans = (((1,), (1,)), ((), ()))
    plain = (((1,), (0,)), ((), ()))
    depth, width = weights.shape[1:]

    def picked(k):
        a = table[0, k]
        o = table[1, k]
        at_a = a + quotient(a, rows_a) * rows_o
        at_o = o + rows_a + quotient(o, rows_o) * rows_a
        live = k < live_count
        ta = band[at_a]
        to = band[at_o]
        ta = jnp.where(live, ta, jnp.zeros_like(ta))
        to = jnp.where(live, to, jnp.zeros_like(to))
        return at_a, at_o, ta, to

    for k in range(0, pairs, 2):
        first, second = picked(k), picked(k + 1)
        both = weights[k : k + 2].reshape(2 * depth, width)
        none = jnp.zeros_like(first[2])
        left = jnp.concatenate([first[2], none], axis=0)
        right = jnp.concatenate([none, second[2]], axis=0)
        ahead = lax.dot_general(
            jnp.concatenate([left, right], axis=1), both, plain, preferred_element_type=F32
        )
        back = lax.dot_general(
            jnp.concatenate([first[3], second[3]], axis=0), both, trans, preferred_element_type=F32
        )
        total[first[1]] += ahead[0:SURF]
        total[second[1]] += ahead[SURF:]
        total[first[0]] += back[0:SURF, 0:depth]
        total[second[0]] += back[SURF:, depth:]
    own_out[...] = total[pl.ds(me * block, block)]
    lanes = weights.shape[2]
    for e, ref in zip(targets, outs):
        part = total[pl.ds(e * block, block)].astype(BF16)
        ref[0 : block * SURF, :] = part.reshape(block * SURF, lanes)


def stencil(rows_a, rows_o, lined, rate, even_in, odd_in, atm_out, ocean_out):
    comp = lax.axis_index("comp")
    lanes = lined.shape[2]
    lane = lax.broadcasted_iota(jnp.int32, (8, lanes), 1)
    at_west = lane == 0
    at_east = lane == lanes - 1
    keep_north = jnp.where(comp == 0, 0.0, 1.0).astype(F32)
    keep_south = jnp.where(comp == lax.axis_size("comp") - 1, 0.0, 1.0).astype(F32)
    at = 0
    for rows, out in ((rows_a, atm_out), (rows_o, ocean_out)):
        channels = out.shape[0] // rows
        for c in range(0, channels, 8):
            rho = rate[at + c : at + c + 8, :]
            own = 1.0 - 4.0 * rho
            north, south = halo_rows(comp, even_in, odd_in, at + c)
            q = north + [lined[r, at + c : at + c + 8, :] for r in range(rows)] + south
            p = []
            for i in range(1, rows + 3):
                west = jnp.where(at_west, 0.0, pltpu.roll(q[i], 1, 1))
                east = jnp.where(at_east, 0.0, pltpu.roll(q[i], lanes - 1, 1))
                p.append(own * q[i] + rho * ((q[i - 1] + q[i + 1]) + (west + east)))
            p[0] = p[0] * keep_north
            p[rows + 1] = p[rows + 1] * keep_south
            for r in range(rows):
                ghost = rho * q[r + 2]
                west = jnp.where(at_west, ghost, pltpu.roll(p[r + 1], 1, 1))
                east = jnp.where(at_east, ghost, pltpu.roll(p[r + 1], lanes - 1, 1))
                out[pl.ds(c * rows + r, 8, stride=rows), :] = own * p[r + 1] + rho * (
                    (p[r] + p[r + 2]) + (west + east)
                )
        at += channels


def edges(rows_a, rows_o, mask, rate, atm, ocean, own, got_a, got_b, *refs):
    atm_out, ocean_out, surface, force, north, south, value_a, value_o, done = refs
    channels, lanes = rate.shape
    block = rows_a + rows_o
    message = block * SURF
    tile_parity = lax.rem(lax.axis_index("tile"), 2)
    row = lax.broadcasted_iota(jnp.int32, (8, lanes), 0)
    lane = lax.broadcasted_iota(jnp.int32, (8, lanes), 1)
    east = lax.div(row, 2) == tile_parity
    second = lax.rem(row, 2)
    spot = jnp.where(east, lanes - 1 - second, second)
    place = jnp.where((row < 4) & (lane == spot), 1.0, 0.0).astype(BF16)
    outer = jnp.where(row == tile_parity, lanes - 1, 0)
    place_outer = jnp.where((row < 2) & (lane == outer), 1.0, 0.0).astype(BF16)
    dims = (((0,), (0,)), ((), ()))

    def sides(at, count):
        rows = [got_a[at : at + count, :].astype(F32), got_b[at : at + count, :].astype(F32)]
        rows.append(jnp.zeros((8 - 2 * count, lanes), F32))
        return jnp.concatenate(rows, axis=0).astype(BF16)

    pieces = -(-channels // lanes)
    first = message + 2 * channels // 8
    for side, ref in ((0, north), (1, south)):
        for i in range(pieces):
            size = min(lanes, channels - i * lanes)
            cells = lax.dot_general(
                sides(first + side * pieces + i, 1), place_outer, dims, preferred_element_type=F32
            )
            rho = rate[i * lanes : i * lanes + size, :]
            ref[i * lanes : i * lanes + size, :] = 2.0 * rho * rho * cells[0:size, :]
    group = 32
    at = 0
    copies = []
    for ref, keep, out, rows in (
        (atm, value_a, atm_out, rows_a),
        (ocean, value_o, ocean_out, rows_o),
    ):
        count = ref.shape[0] // rows
        for c in range(0, count, 8):
            keep[c * rows : (c + 8) * rows, :] = ref[
                c * rows : (c + 8) * rows, :
            ] + lax.dot_general(
                sides(message + 2 * ((at + c) // 8), 2), place, dims, preferred_element_type=F32
            )
            top = pl.ds(c * rows, 8, stride=rows)
            bottom = pl.ds(c * rows + rows - 1, 8, stride=rows)
            keep[top, :] = keep[top, :] + north[at + c : at + c + 8, :]
            keep[bottom, :] = keep[bottom, :] + south[at + c : at + c + 8, :]
            if (c + 8) % group == 0 or c + 8 == count:
                begin = max(c // group * group, SURF) * rows
                end = (c + 8) * rows
                copies.append(
                    pltpu.make_async_copy(
                        keep.at[begin:end], out.at[begin:end], done.at[len(copies)]
                    )
                )
                copies[-1].start()
        at += count
    for y in range(block):
        total = own[y]
        for ref in (got_a, got_b):
            total = total + ref[SURF * y : SURF * y + SURF, :].astype(F32)
        if y >= rows_a:
            total = total * mask[0, y - rows_a].astype(F32)
        start = y if y < rows_a else SURF * rows_a + y - rows_a
        force[pl.ds(start, SURF, stride=rows_a if y < rows_a else rows_o), :] = total
    split = SURF * rows_a
    surface[0:split, :] = value_a[0:split, :] + force[0:split, :]
    surface[split:, :] = value_o[0 : SURF * rows_o, :] + force[split:, :]
    for copy in copies:
        copy.wait()


def final(rows_a, rows_o, mask, surface, *refs):
    got = refs[:-7]
    _, _, atm_out, ocean_out, force, value, done = refs[-7:]
    block = rows_a + rows_o
    for y in range(block):
        total = got[0][SURF * y : SURF * y + SURF, :].astype(F32)
        for ref in got[1:]:
            total = total + ref[SURF * y : SURF * y + SURF, :].astype(F32)
        if y >= rows_a:
            total = total * mask[0, y - rows_a].astype(F32)
        start = y if y < rows_a else SURF * rows_a + y - rows_a
        force[pl.ds(start, SURF, stride=rows_a if y < rows_a else rows_o), :] = total
    split = SURF * rows_a
    copies = []
    for i, (begin, end, out) in enumerate(
        ((0, split, atm_out), (split, SURF * block, ocean_out))
    ):
        value[begin:end, :] = surface[begin:end, :] + force[begin:end, :]
        copies.append(
            pltpu.make_async_copy(value.at[begin:end], out.at[0 : end - begin], done.at[i])
        )
        copies[-1].start()
    for copy in copies:
        copy.wait()


def call(body, micros, limit, **rest):
    return pl.pallas_call(
        body,
        compiler_params=pltpu.CompilerParams(vmem_limit_bytes=limit),
        cost_estimate=pl.CostEstimate(
            flops=0, transcendentals=0, bytes_accessed=int(micros * 3.0e6)
        ),
        **rest,
    )


def exchange(blocks, routes):
    out = []
    for block, route in zip(blocks, routes):
        out.append(lax.ppermute(block, "tile", route))
    return out


def interval(
    atm_state,
    ocean_state,
    atm_rate,
    ocean_rate,
    ocean_mask,
    remap_weight,
    pair_src,
    pair_tgt,
    pair_count,
):
    channels_a, rows_a, lanes = atm_state.shape
    channels_o, rows_o, _ = ocean_state.shape
    channels = channels_a + channels_o
    tile_count = lax.axis_size("tile")
    block = rows_a + rows_o
    message = block * SURF
    extra = -(-(2 * channels // 8 + 2 * -(-channels // lanes)) // 16) * 16
    atm = atm_state.reshape(channels_a * rows_a, lanes)
    ocean = ocean_state.reshape(channels_o * rows_o, lanes)
    mask = ocean_mask.reshape(1, rows_o)
    routes = tile_pairs(tile_count)
    even_pairs, odd_pairs = comp_pairs(lax.axis_size("comp"))

    hbm = lambda x: pltpu.with_memory_space_constraint(x, pltpu.HBM)
    surface, rate_a, rate_o, table, wet = call(
        functools.partial(pack_surface, rows_a, rows_o),
        0.8,
        4 << 20,
        in_specs=[HBM] * 7,
        out_specs=[VMEM] * 3 + [SMEM] * 2,
        out_shape=[
            pltpu.VMEM((block, SURF, lanes), BF16),
            pltpu.VMEM((1, channels_a), F32),
            pltpu.VMEM((1, channels_o), F32),
            pltpu.SMEM((2, pair_src.shape[1]), jnp.int32),
            pltpu.SMEM((1, rows_o), jnp.int32),
        ],
        scratch_shapes=[
            pltpu.VMEM((SURF * rows_a, lanes), F32),
            pltpu.VMEM((SURF * rows_o, lanes), F32),
            pltpu.SemaphoreType.DMA((7,)),
        ],
        name="pack_surface",
    )(
        hbm(atm),
        hbm(ocean),
        hbm(mask),
        hbm(pair_src),
        hbm(pair_tgt),
        hbm(atm_rate.reshape(1, channels_a)),
        hbm(ocean_rate.reshape(1, channels_o)),
    )
    received = exchange([surface] * len(routes), routes)

    halo = pltpu.VMEM((2, channels, lanes), BF16)
    even_rows, odd_rows, rate, live = call(
        functools.partial(prepare, rows_a, rows_o),
        0.5,
        4 << 20,
        in_specs=[VMEM, VMEM, SMEM, HBM, VMEM, VMEM],
        out_specs=[VMEM] * 3 + [SMEM],
        out_shape=[
            halo,
            halo,
            pltpu.VMEM((channels, lanes), F32),
            pltpu.SMEM((1, pair_src.shape[1]), jnp.int32),
        ],
        name="prepare",
    )(atm, ocean, pair_count, hbm(remap_weight[0]), rate_a, rate_o)
    even_in = lax.ppermute(even_rows, "comp", even_pairs)
    odd_in = lax.ppermute(odd_rows, "comp", odd_pairs)

    stage, lined = call(
        functools.partial(pack_columns, rows_a, rows_o),
        1.1,
        8 << 20,
        in_specs=[VMEM] * 3,
        out_specs=[VMEM, VMEM],
        out_shape=[
            pltpu.VMEM((2, extra, lanes), F32),
            pltpu.VMEM((max(rows_a, rows_o), channels, lanes), F32),
        ],
        scratch_shapes=[pltpu.VMEM((channels_a * rows_a + channels_o * rows_o, lanes), F32)],
        name="pack_columns",
    )(atm, ocean, rate)

    sends = [jax.ShapeDtypeStruct((message + extra, lanes), BF16)] * 2
    sends += [jax.ShapeDtypeStruct((message, lanes), BF16)] * (tile_count - 3)
    own_part, *parts = call(
        functools.partial(remap, tile_count, rows_a, rows_o),
        2.0,
        12 << 20,
        in_specs=[SMEM, SMEM] + [VMEM] * (1 + tile_count),
        out_specs=[VMEM] * tile_count,
        out_shape=[jax.ShapeDtypeStruct((block, SURF, lanes), F32)] + sends,
        scratch_shapes=[
            pltpu.VMEM((tile_count * block, SURF, lanes), BF16),
            pltpu.VMEM((tile_count * block, SURF, lanes), F32),
        ],
        name="remap",
    )(table, live, remap_weight[0], surface, *received)
    parts[:2] = call(
        corners,
        0.3,
        8 << 20,
        in_specs=[VMEM] * 5,
        out_specs=[VMEM, VMEM],
        out_shape=sends[:2],
        input_output_aliases={3: 0, 4: 1},
        scratch_shapes=[pltpu.VMEM((2, extra, lanes), F32)],
        name="corners",
    )(stage, even_in, odd_in, *parts[:2])
    returned = exchange(parts, routes)

    atm_base, ocean_base = call(
        functools.partial(stencil, rows_a, rows_o),
        2.5,
        8 << 20,
        in_specs=[VMEM] * 4,
        out_specs=[VMEM, VMEM],
        out_shape=[
            jax.ShapeDtypeStruct(atm.shape, F32),
            jax.ShapeDtypeStruct(ocean.shape, F32),
        ],
        name="stencil",
    )(lined, rate, even_in, odd_in)

    result = [pltpu.HBM(atm.shape, F32), pltpu.HBM(ocean.shape, F32)]
    atm_next, ocean_next, base = call(
        functools.partial(edges, rows_a, rows_o),
        1.5,
        12 << 20,
        in_specs=[SMEM] + [VMEM] * 6,
        out_specs=[HBM, HBM, VMEM],
        out_shape=result + [pltpu.VMEM((message, lanes), F32)],
        scratch_shapes=[
            pltpu.VMEM((message, lanes), F32),
            pltpu.VMEM((channels, lanes), F32),
            pltpu.VMEM((channels, lanes), F32),
            pltpu.VMEM(atm.shape, F32),
            pltpu.VMEM(ocean.shape, F32),
            pltpu.SemaphoreType.DMA((channels // 8,)),
        ],
        name="edges",
    )(wet, rate, atm_base, ocean_base, own_part, *returned[:2])
    far = returned[2:]
    atm_next, ocean_next = call(
        functools.partial(final, rows_a, rows_o),
        0.7,
        4 << 20,
        in_specs=[SMEM] + [VMEM] * (1 + len(far)) + [HBM, HBM],
        out_specs=[HBM, HBM],
        out_shape=result,
        input_output_aliases={2 + len(far): 0, 3 + len(far): 1},
        scratch_shapes=[
            pltpu.VMEM((message, lanes), F32),
            pltpu.VMEM((message, lanes), F32),
            pltpu.SemaphoreType.DMA((2,)),
        ],
        name="final",
    )(wet, base, *far, hbm(atm_next), hbm(ocean_next))
    return (
        atm_next.reshape(channels_a, rows_a, lanes),
        ocean_next.reshape(channels_o, rows_o, lanes),
    )


def solution(mesh):
    return jax.shard_map(
        interval,
        mesh=mesh,
        in_specs=(
            P(None, "comp", "tile"),
            P(None, "comp", "tile"),
            P(),
            P(),
            P("comp", "tile"),
            P("comp", "tile", None, None),
            P("comp", "tile"),
            P("comp", "tile"),
            P("comp", "tile"),
        ),
        out_specs=(P(None, "comp", "tile"), P(None, "comp", "tile")),
        check_vma=False,
    )
```
